128 devices in a mesh: prow: 8 (over y, core), pcol: 16 (over x, z).
Axes of the slice: x: 4, y: 4, z: 4, core: 2. Of those that a mesh axis runs over, the one named last changes fastest.
Arguments:
- right_sides: bfloat16 [32768, 128], P(('prow', 'pcol')), may hold values from -6 to 6
- factor: bfloat16 [16, 16, 32, 8, 128, 128], P(None, 'pcol', None, 'prow'), may hold values from -0.046875 to 0.046875
- pattern: int32 [16, 16, 32, 8], P(None, 'pcol', None, 'prow'), may hold values 0 or 1
- lower_inverse: bfloat16 [16, 16, 128, 128], P(None, 'pcol'), may hold values from -0.5 to 0.5
- upper_inverse: bfloat16 [16, 16, 128, 128], P(None, 'pcol'), may hold values from -0.5 to 0.5
Outputs:
- solution: bfloat16 [32768, 128], P(('prow', 'pcol'))
The draws below stay inside these ranges and needn't reach their ends.
All inputs are finite; a program needn't handle non-finite values. No bound on the sum of `pattern` on one device may be relied on, other than what follows from the above.
Results may differ from the reference program's by a relative error of at most 0.02.
Values may be sent and summed in bfloat16 or wider, within the bound.
A program may use at most 128 MiB of HBM per device.

```python
import jax
import jax.numpy as jnp
from jax import lax

S = 128
NRHS = 128
NB = 256
ROWS = 32768
N_PROW = 8
N_PCOL = 16


def set_ends(array, rng, least, top_value):
    extent = array.shape
    spot = [jax.random.randint(jax.random.fold_in(rng, axis), (), 0, extent[axis]) for axis in range(len(extent))]
    array = array.at[tuple(spot)].set(least)
    longest = extent.index(max(extent))
    spot[longest] = (spot[longest] + 1) % extent[longest]
    return array.at[tuple(spot)].set(top_value)


def block_scale(key, extent, shards, low, largest):
    gain = 1.0
    for position, parts in shards:
        heights = jax.random.uniform(jax.random.fold_in(jax.random.fold_in(key, 6), position), (parts,), jnp.float32, low / len(shards), largest / len(shards))
        gain = gain * jnp.repeat(jnp.exp(heights), extent[position] // parts).reshape((-1,) + (1,) * (len(extent) - 1 - position))
    return gain


def bell_draw(rng, shape, scale, most, split=(), kind=jnp.bfloat16):
    values = scale * jax.random.normal(rng, shape, jnp.float32)
    if split:
        values = values * block_scale(rng, shape, split, -0.22, 0.18)
    return jnp.clip(values, -most, most).astype(kind)


def setup_inputs(seed: int = 0) -> dict:
    key_list = jax.random.split(jax.random.key(seed), 6)
    right_sides = bell_draw(key_list[0], (ROWS, NRHS), 1.0, 6.0, ((0, 128),))
    factor = bell_draw(key_list[1], (NB // N_PCOL, N_PCOL, NB // N_PROW, N_PROW, S, S), (NB * S // 2) ** -0.5, 0.046875, ((1, 16), (3, 8)))
    pattern = set_ends((jax.random.randint(key_list[2], (NB // N_PCOL, N_PCOL, NB // N_PROW, N_PROW), 0, 2) < 1).astype(jnp.int32), jax.random.fold_in(key_list[2], 1), 0, 1)
    lower_inverse = bell_draw(key_list[3], (NB // N_PCOL, N_PCOL, S, S), S ** -0.5, 0.5, ((1, 16),))
    upper_inverse = bell_draw(key_list[4], (NB // N_PCOL, N_PCOL, S, S), S ** -0.5, 0.5, ((1, 16),))
    return {"right_sides": right_sides, "factor": factor, "pattern": pattern, "lower_inverse": lower_inverse, "upper_inverse": upper_inverse}


def level_index(index_vals, node_count):
    bounds = (node_count // 2, 3 * node_count // 4, 7 * node_count // 8)
    result = jnp.zeros(index_vals.shape, jnp.int32)
    for edge_val in bounds:
        result = result + (index_vals >= edge_val).astype(jnp.int32)
    return result


def level_terms(row_blocks_all, keep_mask, solved):
    solved_wide = solved.astype(jnp.float32)

    def row_term(pieces):
        row_blocks, row_keep = pieces
        masked = row_blocks.astype(jnp.float32) * row_keep[:, None, None]
        return jnp.einsum("jab,jbn->an", masked, solved_wide, precision=lax.Precision.HIGHEST)

    return lax.map(row_term, (row_blocks_all, keep_mask))


def apply_inverse(inverse_blocks, remainder):
    return jnp.einsum("iab,ibn->ian", inverse_blocks.astype(jnp.float32), remainder.astype(jnp.float32), precision=lax.Precision.HIGHEST).astype(jnp.bfloat16)


def reference(right_sides, factor, pattern, lower_inverse, upper_inverse):
    node_count = NB
    blocks = factor.reshape(node_count, node_count, S, S)
    pattern_mat = pattern.reshape(node_count, node_count)
    lower_mats = lower_inverse.reshape(node_count, S, S)
    upper_mats = upper_inverse.reshape(node_count, S, S)
    right_blocks = right_sides.reshape(node_count, S, NRHS)
    levels = level_index(jnp.arange(node_count, dtype=jnp.int32), node_count)
    bounds = (0, node_count // 2, 3 * node_count // 4, 7 * node_count // 8, node_count)
    forward_vals = jnp.zeros((node_count, S, NRHS), jnp.bfloat16)
    for level_id in range(4):
        row_start, row_end = bounds[level_id], bounds[level_id + 1]
        keep_mask = ((pattern_mat[row_start:row_end] > 0) & (levels[None, :] < level_id)).astype(jnp.float32)
        summed = level_terms(blocks[row_start:row_end], keep_mask, forward_vals)
        remainder = (right_blocks[row_start:row_end].astype(jnp.float32) - summed).astype(jnp.bfloat16)
        remainder = lax.optimization_barrier(remainder)
        solved = apply_inverse(lower_mats[row_start:row_end], remainder)
        forward_vals = forward_vals.at[row_start:row_end].set(solved)
    backward_vals = jnp.zeros((node_count, S, NRHS), jnp.bfloat16)
    for level_id in (3, 2, 1, 0):
        row_start, row_end = bounds[level_id], bounds[level_id + 1]
        keep_mask = ((pattern_mat[row_start:row_end] > 0) & (levels[None, :] > level_id)).astype(jnp.float32)
        summed = level_terms(blocks[row_start:row_end], keep_mask, backward_vals)
        remainder = (forward_vals[row_start:row_end].astype(jnp.float32) - summed).astype(jnp.bfloat16)
        remainder = lax.optimization_barrier(remainder)
        solved = apply_inverse(upper_mats[row_start:row_end], remainder)
        backward_vals = backward_vals.at[row_start:row_end].set(solved)
    return backward_vals.reshape(node_count * S, NRHS)
```

```python
import jax
import jax.numpy as jnp
from jax import lax
from jax.experimental import pallas as pl
from jax.experimental.pallas import tpu as pltpu
from jax.sharding import PartitionSpec as P

MESH = pl.DeviceIdType.MESH
S = 128
BF = jnp.bfloat16
F32 = jnp.float32
NP, NQ = 8, 16

GROUPS = ((8, 16, 0, 16), (12, 16, 16, 24), (14, 16, 24, 28), (12, 14, 28, 32), (8, 12, 24, 32), (0, 8, 16, 32))


def nt(a, b):
    return lax.dot_general(a, b, (((1,), (1,)), ((), ())), preferred_element_type=F32)


def level0_row(p):
    y = p // 2
    return 2 * ((2 * y - y // 2) % 4) + p % 2


def kernel(
    rhs_hbm, factor_hbm, pattern, lower_hbm, upper_hbm, out_ref,
    raw, fm, yt, xt, rhs_v, rhs_t, b0, b1, b2, b3, linv0, linv, uinv,
    ps1, ps2, ps3, ps0, rb1, rb2, rb3, rbb2, rbb1, rb0, psb2, psb1,
    y0s, y1s, y2s, y3s, x3s, x2s, x1s, x0s, y0own, xo, accf, acc1, acc0,
    lsem, gsem, bsem, osem, rs_s, rs_r, mc_s, mc_s0, mc_r, l0_s, l0_r, b_s, b_r, yo_s, yo_r, xo_s, xo_r,
):
    p = lax.axis_index("prow")
    q = lax.axis_index("pcol")
    me = p * NQ + q

    load_rhs = pltpu.make_async_copy(rhs_hbm, rhs_v, lsem)
    load_rhs.start()
    loads = []
    for g, (r0, r1, c0, c1) in enumerate(GROUPS):
        c = pltpu.make_async_copy(
            factor_hbm.at[r0:r1, c0:c1], raw.at[r0:r1, c0:c1], gsem.at[g]
        )
        c.start()
        loads.append(c)
    row1, row2, row3, row0 = 8 + p // 2, 12 + p // 4, 14 + p // 4, level0_row(p)
    inv_loads = []
    for k, r in enumerate((row1, row2, row3)):
        inv_loads.append(pltpu.make_async_copy(lower_hbm.at[r], linv.at[k], bsem.at[k]))
    for k, r in enumerate((row1, row2, row3, row0)):
        inv_loads.append(pltpu.make_async_copy(upper_hbm.at[r], uinv.at[k], bsem.at[3 + k]))
    for c in inv_loads:
        c.start()

    barrier = pltpu.get_barrier_semaphore()

    def greet(k, carry):
        o = (me + k) % (NP * NQ)
        pl.semaphore_signal(barrier, 1, device_id=(o // NQ, o % NQ), device_id_type=MESH)
        return carry

    lax.fori_loop(1, NP * NQ, greet, 0)

    load_rhs.wait()
    for s in range(2):
        rhs_t[s] = rhs_v[s * S:(s + 1) * S, :].astype(F32).T.astype(BF)

    pl.semaphore_wait(barrier, NP * NQ - 1)

    def send(src, dst, ssem, rsem, dp, dq):
        here = (dp == p) & (dq == q)
        remote = pltpu.make_async_remote_copy(
            src_ref=src, dst_ref=dst, send_sem=ssem, recv_sem=rsem, device_id=(dp, dq), device_id_type=MESH
        )

        @pl.when(here)
        def _():
            pltpu.make_async_copy(src, dst, rsem).start()

        @pl.when(jnp.logical_not(here))
        def _():
            remote.start()

        def finish():
            @pl.when(jnp.logical_not(here))
            def _():
                remote.wait_send()

        return finish

    def arrived(ref, sem):
        pltpu.make_async_copy(ref, ref, sem).wait()

    def level0_q(jb):
        return (jb % 4) * 4 + jb // 4

    owner = q % NP == p

    @pl.when(owner)
    def _():
        for r in range(8):
            send(lower_hbm.at[r], linv0, l0_s.at[r], l0_r, p, level0_q(2 * r + q // 8))

    @pl.when(p < 4)
    def _():
        for s in range(2):
            n = 2 * me + s
            send(rhs_t.at[s], b0, b_s.at[s], b_r.at[0], n % 8, level0_q(n // 8))

    @pl.when((p >= 4) & (p < 6))
    def _():
        for s in range(2):
            n = 2 * me + s
            for h in range(2):
                send(rhs_t.at[s, pl.ds(64 * h, 64)], b1, b_s.at[2 * s + h], b_r.at[1], 2 * (n // 16 - 8) + h, n % 16)

    for lev, (at_p, dst) in enumerate(((6, b2), (7, b3))):
        @pl.when(p == at_p)
        def _():
            for s in range(2):
                n = 2 * me + s
                for c in range(4):
                    send(
                        rhs_t.at[s, pl.ds(32 * c, 32)], dst, b_s.at[4 * s + c], b_r.at[2 + lev],
                        4 * (n // 16 - 12 - 2 * lev) + c, n % 16,
                    )

    def mask_group(g):
        r0, r1, c0, c1 = GROUPS[g]
        loads[g].wait()

        def row(i, carry):
            for j in range(c0, c1):
                keep = jnp.where(pattern[i, j] > 0, 1.0, 0.0).astype(F32)
                m = jnp.full((S, S), keep, F32).astype(BF)
                fm[pl.ds(pl.multiple_of(i * S, S), S), j * S:(j + 1) * S] = raw[i, j] * m
            return carry

        lax.fori_loop(r0, r1, row, 0)

    mask_group(0)

    def multicast(idx, stage, buf, col, n0, rows, tp):
        dst = buf.at[pl.ds(n0, rows), pl.ds(pl.multiple_of(col * S, S), S)]
        first = send(stage, dst, mc_s0.at[idx], mc_r.at[idx], tp, q)

        def one(k, carry):
            pltpu.make_async_remote_copy(
                src_ref=stage, dst_ref=dst, send_sem=mc_s.at[idx], recv_sem=mc_r.at[idx],
                device_id=(tp, (q + k) % NQ), device_id_type=MESH,
            ).start()
            return carry

        lax.fori_loop(1, NQ, one, 0)

        def finish():
            first()
            ref = fm.at[0:(NQ - 1) * rows, 0:S]
            arrived(ref, mc_s.at[idx])

        return finish

    def exchange(idx, ps, rb):
        for k in range(1, NP):
            d = (p + k) % NP
            pltpu.make_async_remote_copy(
                src_ref=ps.at[d], dst_ref=rb.at[k - 1], send_sem=rs_s.at[idx], recv_sem=rs_r.at[idx],
                device_id=(d, q), device_id_type=MESH,
            ).start()

        def finish():
            arrived(rb, rs_s.at[idx])

        return finish

    def summed(idx, ps, rb):
        arrived(rb, rs_r.at[idx])
        total = ps[p].astype(F32)
        for k in range(NP - 1):
            total = total + rb[k].astype(F32)
        return total

    def split(part, ps, per_row, rows):
        for d in range(NP):
            r, c = d // per_row, d % per_row
            ps[d] = part[c * rows:(c + 1) * rows, r * S:(r + 1) * S].astype(BF)

    tp = q % NP
    hi = q // NP
    done = []

    arrived(b0, b_r.at[0])
    arrived(linv0, l0_r)
    y0s[...] = nt(b0[...], linv0[...]).astype(BF)
    done.append(multicast(0, y0s, yt, (q % 4) * 4 + q // 4, 0, S, p))
    mask_group(1)
    mask_group(2)
    arrived(yt.at[:, 0:16 * S], mc_r.at[0])

    split(nt(yt[:, 0:16 * S], fm[8 * S:12 * S, 0:16 * S]), ps1, 2, 64)
    done.append(exchange(0, ps1, rb1))

    @pl.when(owner)
    def _():
        for d in range(NP):
            col = 2 * level0_row(d) + hi
            send(yt.at[:, pl.ds(pl.multiple_of(col * S, S), S)], y0own, yo_s.at[d], yo_r, d, q)

    accf[...] = nt(yt[:, 0:16 * S], fm[12 * S:16 * S, 0:16 * S])
    for c in inv_loads:
        c.wait()
    arrived(b1, b_r.at[1])
    e = (b1[...].astype(F32) - summed(0, ps1, rb1)).astype(BF)
    y1s[...] = nt(e, linv[0]).astype(BF)
    n1 = pl.multiple_of((p % 2) * 64, 64)
    n2 = pl.multiple_of((p % 4) * 32, 32)
    done.append(multicast(1, y1s, yt, 2 * row1 + hi, n1, 64, tp))
    for g in (3, 4, 5):
        mask_group(g)
    arrived(yt.at[:, 16 * S:24 * S], mc_r.at[1])

    split(accf[:, 0:2 * S] + nt(yt[:, 16 * S:24 * S], fm[12 * S:14 * S, 16 * S:24 * S]), ps2, 4, 32)
    done.append(exchange(1, ps2, rb2))
    accf[:, 2 * S:4 * S] += nt(yt[:, 16 * S:24 * S], fm[14 * S:16 * S, 16 * S:24 * S])
    arrived(b2, b_r.at[2])
    e = (b2[...].astype(F32) - summed(1, ps2, rb2)).astype(BF)
    y2s[...] = nt(e, linv[1]).astype(BF)
    done.append(multicast(2, y2s, yt, 2 * row2 + hi, n2, 32, tp))
    arrived(yt.at[:, 24 * S:28 * S], mc_r.at[2])

    split(accf[:, 2 * S:4 * S] + nt(yt[:, 24 * S:28 * S], fm[14 * S:16 * S, 24 * S:28 * S]), ps3, 4, 32)
    done.append(exchange(2, ps3, rb3))
    arrived(b3, b_r.at[3])
    e = (b3[...].astype(F32) - summed(2, ps3, rb3)).astype(BF)
    y3s[...] = nt(e, linv[2]).astype(BF)
    x3s[...] = nt(y3s[...], uinv[2]).astype(BF)
    done.append(multicast(3, x3s, xt, 2 * row3 + hi - 16, n2, 32, tp))
    done.append(send(x3s, xo.at[q % 2, pl.ds(n2, 32)], xo_s.at[3], xo_r, 7, 8 * (row3 % 2) + q // 2))
    arrived(xt.at[:, 12 * S:16 * S], mc_r.at[3])

    split(nt(xt[:, 12 * S:16 * S], fm[12 * S:14 * S, 28 * S:32 * S]), psb2, 4, 32)
    done.append(exchange(3, psb2, rbb2))
    acc1[...] = nt(xt[:, 12 * S:16 * S], fm[8 * S:12 * S, 28 * S:32 * S])
    acc0[...] = nt(xt[:, 12 * S:16 * S], fm[0:8 * S, 28 * S:32 * S])
    g = (y2s[...].astype(F32) - summed(3, psb2, rbb2)).astype(BF)
    x2s[...] = nt(g, uinv[1]).astype(BF)
    done.append(multicast(4, x2s, xt, 2 * row2 + hi - 16, n2, 32, tp))
    done.append(send(x2s, xo.at[q % 2, pl.ds(n2, 32)], xo_s.at[2], xo_r, 6, 8 * (row2 % 2) + q // 2))
    arrived(xt.at[:, 8 * S:12 * S], mc_r.at[4])

    split(acc1[...] + nt(xt[:, 8 * S:12 * S], fm[8 * S:12 * S, 24 * S:28 * S]), psb1, 2, 64)
    done.append(exchange(4, psb1, rbb1))
    acc0[...] += nt(xt[:, 8 * S:12 * S], fm[0:8 * S, 24 * S:28 * S])
    g = (y1s[...].astype(F32) - summed(4, psb1, rbb1)).astype(BF)
    x1s[...] = nt(g, uinv[0]).astype(BF)
    done.append(multicast(5, x1s, xt, 2 * row1 + hi - 16, n1, 64, tp))
    done.append(send(x1s, xo.at[q % 2, pl.ds(n1, 64)], xo_s.at[1], xo_r, row1 // 2, 8 * (row1 % 2) + q // 2))
    arrived(xt.at[:, 0:8 * S], mc_r.at[5])

    part = acc0[...] + nt(xt[:, 0:8 * S], fm[0:8 * S, 16 * S:24 * S])
    for d in range(NP):
        r = level0_row(d)
        ps0[d] = part[:, r * S:(r + 1) * S].astype(BF)
    done.append(exchange(5, ps0, rb0))
    arrived(y0own, yo_r)
    g = (y0own[...].astype(F32) - summed(5, ps0, rb0)).astype(BF)
    x0s[...] = nt(g, uinv[3]).astype(BF)
    done.append(send(x0s, xo.at[q % 2], xo_s.at[0], xo_r, row0 // 2, 8 * (row0 % 2) + q // 2))
    arrived(xo, xo_r)
    for s in range(2):
        out_ref[s * S:(s + 1) * S, :] = xo[s].astype(F32).T.astype(BF)

    for f in done:
        f()

    @pl.when(owner)
    def _():
        for r in range(8):
            dq = level0_q(2 * r + q // 8)

            @pl.when(dq != q)
            def _():
                arrived(linv0, l0_s.at[r])

        for d in range(NP):
            @pl.when(d != p)
            def _():
                arrived(y0own, yo_s.at[d])

    @pl.when(p < 4)
    def _():
        for s in range(2):
            n = 2 * me + s

            @pl.when(jnp.logical_not((n % 8 == p) & (level0_q(n // 8) == q)))
            def _():
                arrived(b0, b_s.at[s])

    @pl.when((p >= 4) & (p < 6))
    def _():
        for s in range(2):
            n = 2 * me + s
            for h in range(2):
                @pl.when(jnp.logical_not((2 * (n // 16 - 8) + h == p) & (n % 16 == q)))
                def _():
                    arrived(b1, b_s.at[2 * s + h])

    for lev, (at_p, dst) in enumerate(((6, b2), (7, b3))):
        @pl.when(p == at_p)
        def _():
            for s in range(2):
                n = 2 * me + s
                for c in range(4):
                    @pl.when(jnp.logical_not((4 * (n // 16 - 12 - 2 * lev) + c == p) & (n % 16 == q)))
                    def _():
                        arrived(dst, b_s.at[4 * s + c])


def on_device(right_sides, factor, pattern, lower_inverse, upper_inverse):
    vm = pltpu.VMEM
    dma = pltpu.SemaphoreType.DMA
    hbm = pl.BlockSpec(memory_space=pl.ANY)
    return pl.pallas_call(
        kernel,
        out_shape=jax.ShapeDtypeStruct(right_sides.shape, BF),
        in_specs=[hbm, hbm, pl.BlockSpec(memory_space=pltpu.SMEM), hbm, hbm],
        out_specs=pl.BlockSpec(memory_space=pltpu.VMEM),
        scratch_shapes=[
            vm((16, 32, S, S), BF), vm((16 * S, 32 * S), BF), vm((S, 28 * S), BF), vm((S, 16 * S), BF),
            vm((2 * S, S), BF), vm((2, S, S), BF),
            vm((S, S), BF), vm((64, S), BF), vm((32, S), BF), vm((32, S), BF),
            vm((S, S), BF), vm((3, S, S), BF), vm((4, S, S), BF),
            vm((8, 64, S), BF), vm((8, 32, S), BF), vm((8, 32, S), BF), vm((8, S, S), BF),
            vm((7, 64, S), BF), vm((7, 32, S), BF), vm((7, 32, S), BF), vm((7, 32, S), BF), vm((7, 64, S), BF),
            vm((7, S, S), BF), vm((8, 32, S), BF), vm((8, 64, S), BF),
            vm((S, S), BF), vm((64, S), BF), vm((32, S), BF), vm((32, S), BF),
            vm((32, S), BF), vm((32, S), BF), vm((64, S), BF), vm((S, S), BF),
            vm((S, S), BF), vm((2, S, S), BF),
            vm((S, 4 * S), F32), vm((S, 4 * S), F32), vm((S, 8 * S), F32),
            dma, dma((6,)), dma((7,)), dma, dma((6,)), dma((6,)), dma((6,)), dma((6,)), dma((6,)),
            dma((8,)), dma, dma((8,)), dma((4,)), dma((8,)), dma, dma((4,)), dma,
        ],
        compiler_params=pltpu.CompilerParams(
            collective_id=0, has_side_effects=True, vmem_limit_bytes=60 * 1024 * 1024
        ),
    )(
        right_sides,
        factor.reshape(16, 32, S, S),
        pattern.reshape(16, 32),
        lower_inverse.reshape(16, S, S),
        upper_inverse.reshape(16, S, S),
    )


def solution(mesh):
    return jax.shard_map(
        on_device,
        mesh=mesh,
        in_specs=(
            P(("prow", "pcol"), None),
            P(None, "pcol", None, "prow", None, None),
            P(None, "pcol", None, "prow"),
            P(None, "pcol", None, None),
            P(None, "pcol", None, None),
        ),
        out_specs=P(("prow", "pcol"), None),
        check_vma=False,
    )
```

```python
import jax
import jax.numpy as jnp
from jax import lax
from jax.experimental import pallas as pl
from jax.experimental.pallas import tpu as pltpu
from jax.sharding import PartitionSpec as P

MESH = pl.DeviceIdType.MESH
S = 128
H = 64
BF = jnp.bfloat16
F32 = jnp.float32
NP, NQ = 8, 16

GROUPS = ((8, 16, 0, 16), (12, 16, 16, 24), (14, 16, 24, 28), (12, 14, 28, 32), (8, 12, 24, 32), (0, 8, 16, 32))
STEPS = sorted(
    ((dx, dz) for dx in range(4) for dz in range(4) if dx or dz),
    key=lambda s: -(min(s[0], 4 - s[0]) + min(s[1], 4 - s[1])),
)


def nt(a, b):
    return lax.dot_general(a, b, (((1,), (1,)), ((), ())), preferred_element_type=F32)


def level0_row(p):
    y = p // 2
    return 2 * ((2 * y - y // 2) % 4) + p % 2


def kernel(
    rhs_hbm, factor_hbm, pattern, lower_hbm, upper_hbm, out_ref,
    raw, fm, yt, xt, rhs_v, rhs_t, b0, bx, b1, b2, b3, linv0, linv, uinv,
    ps1, ps2, ps3, psb2, psb1, ps0, rb1, rb2, rb3, rbb2, rbb1, rb0,
    y0s, y1s, y2s, y3s, x3s, x2s, x1s, x0s, y0own, xo, accf, acc1, acc0,
    lsem, gsem, isem, rs_s, rs_r, mc_s, mc_s0, mc_r, l0_s, l0_r, b_s, b0_r, bx_r, bl_s, bl_r, yo_s, yo_r, xo_s, xo_r,
):
    p = lax.axis_index("prow")
    q = lax.axis_index("pcol")
    x, z = q // 4, q % 4
    me = p * NQ + q
    row1, row2, row3, row0 = 8 + p // 2, 12 + p // 4, 14 + p // 4, level0_row(p)

    barrier = pltpu.get_barrier_semaphore()

    def greet(dp, dq):
        pl.semaphore_signal(barrier, 1, device_id=(dp, dq), device_id_type=MESH)

    for dx, dz in STEPS:
        greet(p, (x + dx) % 4 * 4 + (z + dz) % 4)
    for k in range(1, NP):
        greet((p + k) % NP, q)
    corner = (p == 0) & (z == 0)

    @pl.when(jnp.logical_not(corner))
    def _():
        greet(z, x * 4 + p // 2)

    load_rhs = pltpu.make_async_copy(rhs_hbm, rhs_v, lsem)
    load_rhs.start()
    loads = []
    for g, (r0, r1, c0, c1) in enumerate(GROUPS):
        c = pltpu.make_async_copy(factor_hbm.at[r0:r1, c0:c1], raw.at[r0:r1, c0:c1], gsem.at[g])
        c.start()
        loads.append(c)
    inv_loads = []
    for k, r in enumerate((row1, row2, row3)):
        inv_loads.append(pltpu.make_async_copy(lower_hbm.at[r], linv.at[k], isem.at[k]))
    for k, r in enumerate((row1, row2, row3, row0)):
        inv_loads.append(pltpu.make_async_copy(upper_hbm.at[r], uinv.at[k], isem.at[3 + k]))
    for c in inv_loads:
        c.start()

    load_rhs.wait()
    for s in range(2):
        rhs_t[s] = rhs_v[s * S:(s + 1) * S, :].astype(F32).T.astype(BF)

    pl.semaphore_wait(
        barrier, 22 + jnp.where(p < 4, 2, 0) - jnp.where(corner, 1, 0)
    )

    def arrived(ref, sem):
        pltpu.make_async_copy(ref, ref, sem).wait()

    def send(src, dst, ssem, rsem, dp, dq):
        here = (dp == p) & (dq == q)

        @pl.when(here)
        def _():
            pltpu.make_async_copy(src, dst, rsem).start()

        @pl.when(jnp.logical_not(here))
        def _():
            pltpu.make_async_remote_copy(
                src_ref=src, dst_ref=dst, send_sem=ssem, recv_sem=rsem, device_id=(dp, dq), device_id_type=MESH
            ).start()

        def finish():
            @pl.when(jnp.logical_not(here))
            def _():
                arrived(src, ssem)

        return finish

    tp, hi = q % NP, q // NP
    owner = tp == p

    def level0_q(jb):
        return (jb % 4) * 4 + jb // 4

    @pl.when(owner)
    def _():
        for r in range(8):
            send(lower_hbm.at[r], linv0, l0_s.at[r], l0_r, p, level0_q(2 * r + hi))

    for s in range(2):
        @pl.when(p < 4)
        def _():
            send(rhs_t.at[s], b0, b_s.at[s], b0_r, 2 * z + s, x * 4 + p)

        @pl.when(p >= 4)
        def _():
            send(rhs_t.at[s], bx.at[hi], b_s.at[s], bx_r, p, 2 * tp + s)

    def spread_rhs(finish):
        for at, count, dst, sem in ((4, 2, b1, 0), (5, 2, b1, 0), (6, 4, b2, 1), (7, 4, b3, 2)):
            @pl.when(p == at)
            def _():
                for slot in range(2):
                    r = 2 * at + slot - (8, 12, 14)[sem]
                    rows = H // count
                    for c in range(count):
                        for h in range(2):
                            src = bx.at[slot, pl.ds(h * H + c * rows, rows)]
                            d = count * r + c
                            ssem = bl_s.at[(slot * count + c) * 2 + h]
                            if finish:
                                @pl.when(p != d)
                                def _():
                                    arrived(src, ssem)
                            else:
                                send(src, dst.at[h], ssem, bl_r.at[sem], d, q)

    def mask_group(g):
        r0, r1, c0, c1 = GROUPS[g]
        loads[g].wait()

        def row(i, carry):
            for j in range(c0, c1):
                keep = jnp.where(pattern[i, j] > 0, 1.0, 0.0).astype(F32)
                m = jnp.full((S, S), keep, F32).astype(BF)
                fm[pl.ds(pl.multiple_of(i * S, S), S), j * S:(j + 1) * S] = raw[i, j] * m
            return carry

        lax.fori_loop(r0, r1, row, 0)

    mask_group(0)
    done = []

    def multicast(h, idx, stage, buf, col, n0, rows, to):
        dst = buf.at[h, pl.ds(n0, rows), pl.ds(pl.multiple_of(col * S, S), S)]
        for dx, dz in STEPS:
            pltpu.make_async_remote_copy(
                src_ref=stage, dst_ref=dst, send_sem=mc_s.at[h, idx], recv_sem=mc_r.at[h, idx],
                device_id=(to, (x + dx) % 4 * 4 + (z + dz) % 4), device_id_type=MESH,
            ).start()
        first = send(stage, dst, mc_s0.at[h, idx], mc_r.at[h, idx], to, q)

        def finish():
            first()
            arrived(fm.at[0:(NQ - 1) * rows, 0:S], mc_s.at[h, idx])

        done.append(finish)

    def exchange(h, idx, ps, rb):
        for k in (4, 5, 3, 2, 6, 7, 1):
            d = (p + k) % NP
            pltpu.make_async_remote_copy(
                src_ref=ps.at[h, d], dst_ref=rb.at[h, k - 1], send_sem=rs_s.at[h, idx], recv_sem=rs_r.at[h, idx],
                device_id=(d, q), device_id_type=MESH,
            ).start()
        done.append(lambda: arrived(rb.at[h], rs_s.at[h, idx]))

    def summed(h, idx, ps, rb):
        arrived(rb.at[h], rs_r.at[h, idx])
        total = ps[h, p].astype(F32)
        for k in range(NP - 1):
            total = total + rb[h, k].astype(F32)
        return total

    def split(h, part, ps, per_row):
        rows = H // per_row
        for d in range(NP):
            r, c = d // per_row, d % per_row
            ps[h, d] = part[c * rows:(c + 1) * rows, r * S:(r + 1) * S].astype(BF)

    def cols(ref, h, c0, c1):
        return ref[h, :, c0 * S:c1 * S]

    def blocks(r0, r1, c0, c1):
        return fm[r0 * S:r1 * S, c0 * S:c1 * S]

    def to_output(h, lev, stage, slot_row, n0, rows):
        done.append(send(
            stage, xo.at[q % 2, pl.ds(h * H + n0, rows)], xo_s.at[h, lev], xo_r, slot_row // 2, 8 * (slot_row % 2) + q // 2
        ))

    n1 = pl.multiple_of((p % 2) * 32, 32)
    n2 = pl.multiple_of((p % 4) * 16, 16)

    def chain(h):
        lead = h == 0
        if lead:
            arrived(b0, b0_r)
            arrived(linv0, l0_r)
        y0s[h] = nt(b0[h * H:(h + 1) * H, :], linv0[...]).astype(BF)
        multicast(h, 0, y0s.at[h], yt, z * 4 + x, 0, H, p)
        yield
        if lead:
            @pl.when(p >= 4)
            def _():
                arrived(bx, bx_r)
            spread_rhs(False)
            mask_group(1)
            mask_group(2)
        arrived(yt.at[h, :, 0:16 * S], mc_r.at[h, 0])
        split(h, nt(cols(yt, h, 0, 16), blocks(8, 12, 0, 16)), ps1, 2)
        exchange(h, 0, ps1, rb1)
        yield
        @pl.when(owner)
        def _():
            for d in range(NP):
                col = 2 * level0_row(d) + hi
                send(yt.at[h, :, pl.ds(pl.multiple_of(col * S, S), S)], y0own.at[h], yo_s.at[h, d], yo_r.at[h], d, q)

        accf[h] = nt(cols(yt, h, 0, 16), blocks(12, 16, 0, 16))
        if lead:
            for c in inv_loads:
                c.wait()
            arrived(b1, bl_r.at[0])
        e = (b1[h].astype(F32) - summed(h, 0, ps1, rb1)).astype(BF)
        y1s[h] = nt(e, linv[0]).astype(BF)
        multicast(h, 1, y1s.at[h], yt, 2 * row1 + hi, n1, 32, tp)
        yield
        if lead:
            for g in (3, 4, 5):
                mask_group(g)
        arrived(yt.at[h, :, 16 * S:24 * S], mc_r.at[h, 1])
        split(h, accf[h, :, 0:2 * S] + nt(cols(yt, h, 16, 24), blocks(12, 14, 16, 24)), ps2, 4)
        exchange(h, 1, ps2, rb2)
        yield
        accf[h, :, 2 * S:4 * S] += nt(cols(yt, h, 16, 24), blocks(14, 16, 16, 24))
        if lead:
            arrived(b2, bl_r.at[1])
        e = (b2[h].astype(F32) - summed(h, 1, ps2, rb2)).astype(BF)
        y2s[h] = nt(e, linv[1]).astype(BF)
        multicast(h, 2, y2s.at[h], yt, 2 * row2 + hi, n2, 16, tp)
        yield
        arrived(yt.at[h, :, 24 * S:28 * S], mc_r.at[h, 2])
        split(h, accf[h, :, 2 * S:4 * S] + nt(cols(yt, h, 24, 28), blocks(14, 16, 24, 28)), ps3, 4)
        exchange(h, 2, ps3, rb3)
        yield
        if lead:
            arrived(b3, bl_r.at[2])
        e = (b3[h].astype(F32) - summed(h, 2, ps3, rb3)).astype(BF)
        y3s[h] = nt(e, linv[2]).astype(BF)
        x3s[h] = nt(y3s[h], uinv[2]).astype(BF)
        multicast(h, 3, x3s.at[h], xt, 2 * row3 + hi - 16, n2, 16, tp)
        to_output(h, 3, x3s.at[h], row3, n2, 16)
        yield
        arrived(xt.at[h, :, 12 * S:16 * S], mc_r.at[h, 3])
        split(h, nt(cols(xt, h, 12, 16), blocks(12, 14, 28, 32)), psb2, 4)
        exchange(h, 3, psb2, rbb2)
        yield
        acc1[h] = nt(cols(xt, h, 12, 16), blocks(8, 12, 28, 32))
        acc0[h] = nt(cols(xt, h, 12, 16), blocks(0, 8, 28, 32))
        g = (y2s[h].astype(F32) - summed(h, 3, psb2, rbb2)).astype(BF)
        x2s[h] = nt(g, uinv[1]).astype(BF)
        multicast(h, 4, x2s.at[h], xt, 2 * row2 + hi - 16, n2, 16, tp)
        to_output(h, 2, x2s.at[h], row2, n2, 16)
        yield
        arrived(xt.at[h, :, 8 * S:12 * S], mc_r.at[h, 4])
        split(h, acc1[h] + nt(cols(xt, h, 8, 12), blocks(8, 12, 24, 28)), psb1, 2)
        exchange(h, 4, psb1, rbb1)
        yield
        acc0[h] += nt(cols(xt, h, 8, 12), blocks(0, 8, 24, 28))
        g = (y1s[h].astype(F32) - summed(h, 4, psb1, rbb1)).astype(BF)
        x1s[h] = nt(g, uinv[0]).astype(BF)
        multicast(h, 5, x1s.at[h], xt, 2 * row1 + hi - 16, n1, 32, tp)
        to_output(h, 1, x1s.at[h], row1, n1, 32)
        yield
        arrived(xt.at[h, :, 0:8 * S], mc_r.at[h, 5])
        part = acc0[h] + nt(cols(xt, h, 0, 8), blocks(0, 8, 16, 24))
        for d in range(NP):
            r = level0_row(d)
            ps0[h, d] = part[:, r * S:(r + 1) * S].astype(BF)
        exchange(h, 5, ps0, rb0)
        yield
        arrived(y0own.at[h], yo_r.at[h])
        g = (y0own[h].astype(F32) - summed(h, 5, ps0, rb0)).astype(BF)
        x0s[h] = nt(g, uinv[3]).astype(BF)
        to_output(h, 0, x0s.at[h], row0, 0, H)
        yield

    chains = [chain(0), chain(1)]
    while chains:
        for c in list(chains):
            try:
                next(c)
            except StopIteration:
                chains.remove(c)

    arrived(xo, xo_r)
    for s in range(2):
        out_ref[s * S:(s + 1) * S, :] = xo[s].astype(F32).T.astype(BF)

    for f in done:
        f()

    @pl.when(owner)
    def _():
        for r in range(8):
            @pl.when(level0_q(2 * r + hi) != q)
            def _():
                arrived(linv0, l0_s.at[r])

        for d in range(NP):
            @pl.when(d != p)
            def _():
                for h in range(2):
                    arrived(y0own.at[h], yo_s.at[h, d])

    for s in range(2):
        @pl.when((p < 4) & jnp.logical_not((2 * z + s == p) & (p == z)))
        def _():
            arrived(b0, b_s.at[s])

        @pl.when((p >= 4) & (2 * tp + s != q))
        def _():
            arrived(b0, b_s.at[s])

    spread_rhs(True)


def on_device(right_sides, factor, pattern, lower_inverse, upper_inverse):
    def vm(*shape, dtype=BF):
        return pltpu.VMEM(shape, dtype)

    dma = pltpu.SemaphoreType.DMA
    hbm = pl.BlockSpec(memory_space=pl.ANY)
    return pl.pallas_call(
        kernel,
        out_shape=jax.ShapeDtypeStruct(right_sides.shape, BF),
        in_specs=[hbm, hbm, pl.BlockSpec(memory_space=pltpu.SMEM), hbm, hbm],
        out_specs=pl.BlockSpec(memory_space=pltpu.VMEM),
        scratch_shapes=[
            vm(16, 32, S, S), vm(16 * S, 32 * S), vm(2, H, 28 * S), vm(2, H, 16 * S),
            vm(2 * S, S), vm(2, S, S),
            vm(S, S), vm(2, S, S), vm(2, 32, S), vm(2, 16, S), vm(2, 16, S),
            vm(S, S), vm(3, S, S), vm(4, S, S),
            vm(2, 8, 32, S), vm(2, 8, 16, S), vm(2, 8, 16, S), vm(2, 8, 16, S), vm(2, 8, 32, S), vm(2, 8, H, S),
            vm(2, 7, 32, S), vm(2, 7, 16, S), vm(2, 7, 16, S), vm(2, 7, 16, S), vm(2, 7, 32, S), vm(2, 7, H, S),
            vm(2, H, S), vm(2, 32, S), vm(2, 16, S), vm(2, 16, S),
            vm(2, 16, S), vm(2, 16, S), vm(2, 32, S), vm(2, H, S),
            vm(2, H, S), vm(2, S, S),
            vm(2, H, 4 * S, dtype=F32), vm(2, H, 4 * S, dtype=F32), vm(2, H, 8 * S, dtype=F32),
            dma, dma((6,)), dma((7,)), dma((2, 6)), dma((2, 6)), dma((2, 6)), dma((2, 6)), dma((2, 6)),
            dma((8,)), dma, dma((2,)), dma, dma, dma((16,)), dma((3,)), dma((2, 8)), dma((2,)), dma((2, 4)), dma,
        ],
        compiler_params=pltpu.CompilerParams(
            collective_id=0, has_side_effects=True, vmem_limit_bytes=60 * 1024 * 1024
        ),
    )(
        right_sides,
        factor.reshape(16, 32, S, S),
        pattern.reshape(16, 32),
        lower_inverse.reshape(16, S, S),
        upper_inverse.reshape(16, S, S),
    )


def solution(mesh):
    return jax.shard_map(
        on_device,
        mesh=mesh,
        in_specs=(
            P(("prow", "pcol"), None),
            P(None, "pcol", None, "prow", None, None),
            P(None, "pcol", None, "prow"),
            P(None, "pcol", None, None),
            P(None, "pcol", None, None),
        ),
        out_specs=P(("prow", "pcol"), None),
        check_vma=False,
    )
```

```python
import jax
import jax.numpy as jnp
from jax import lax
from jax.experimental import pallas as pl
from jax.experimental.pallas import tpu as pltpu
from jax.sharding import PartitionSpec as P

MESH = pl.DeviceIdType.MESH
S = 128
H = 64
BF = jnp.bfloat16
F32 = jnp.float32
NP, NQ = 8, 16

GROUPS = ((14, 16, 24, 28), (8, 16, 0, 16), (12, 16, 16, 24), (12, 14, 28, 32), (8, 12, 24, 32), (0, 8, 16, 32))
STEPS = sorted(
    ((dx, dz) for dx in range(4) for dz in range(4) if dx or dz),
    key=lambda s: -(min(s[0], 4 - s[0]) + min(s[1], 4 - s[1])),
)


def nt(a, b):
    return lax.dot_general(a, b, (((1,), (1,)), ((), ())), preferred_element_type=F32)


def level0_row(p):
    y = p // 2
    return 2 * ((2 * y - y // 2) % 4) + p % 2


def kernel(
    rhs_hbm, factor_hbm, pattern, lower_hbm, upper_hbm, out_ref,
    raw, fm, yt, xt, rhs_v, rhs_t, b0, bx, b1, b2, b3, linv0, linv, uinv,
    ps1, ps2, ps3, psb1, ps0, rb1, rb2, rb3, rbb1, rb0, up, down, y2p, x3p,
    y0s, y1s, y2s, y3s, x3s, x2s, x1s, x0s, y0own, xo, accf, acc1, acc0,
    lsem, gsem, isem, up_s, up_r, rs_s, rs_r, mc_s, mc_s0, mc_r, l0_s, l0_r, b_s, b0_r, bx_r, bl_s, bl_r, yo_s, yo_r, xo_s, xo_r,
):
    p = lax.axis_index("prow")
    q = lax.axis_index("pcol")
    x, z = q // 4, q % 4
    me = p * NQ + q
    row1, row2, row3, row0 = 8 + p // 2, 12 + p % 2, 14 + p % 2, level0_row(p)

    barrier = pltpu.get_barrier_semaphore()

    def greet(dp, dq):
        pl.semaphore_signal(barrier, 1, device_id=(dp, dq), device_id_type=MESH)

    for dx, dz in STEPS:
        greet(p, (x + dx) % 4 * 4 + (z + dz) % 4)
    for k in range(1, NP):
        greet((p + k) % NP, q)
    corner = (p == 0) & (z == 0)

    @pl.when(jnp.logical_not(corner))
    def _():
        greet(z, x * 4 + p // 2)

    load_rhs = pltpu.make_async_copy(rhs_hbm, rhs_v, lsem)
    load_rhs.start()
    loads = []
    for g, (r0, r1, c0, c1) in enumerate(GROUPS):
        c = pltpu.make_async_copy(factor_hbm.at[r0:r1, c0:c1], raw.at[r0:r1, c0:c1], gsem.at[g])
        c.start()
        loads.append(c)
    inv_loads = []
    for k, r in enumerate((row1, row2, row3)):
        inv_loads.append(pltpu.make_async_copy(lower_hbm.at[r], linv.at[k], isem.at[k]))
    for k, r in enumerate((row1, row2, row3, row0)):
        inv_loads.append(pltpu.make_async_copy(upper_hbm.at[r], uinv.at[k], isem.at[3 + k]))
    for c in inv_loads:
        c.start()

    load_rhs.wait()
    for s in range(2):
        rhs_t[s] = rhs_v[s * S:(s + 1) * S, :].astype(F32).T.astype(BF)

    pl.semaphore_wait(
        barrier, 22 + jnp.where(p < 4, 2, 0) - jnp.where(corner, 1, 0)
    )

    def arrived(ref, sem):
        pltpu.make_async_copy(ref, ref, sem).wait()

    def send(src, dst, ssem, rsem, dp, dq):
        here = (dp == p) & (dq == q)

        @pl.when(here)
        def _():
            pltpu.make_async_copy(src, dst, rsem).start()

        @pl.when(jnp.logical_not(here))
        def _():
            pltpu.make_async_remote_copy(
                src_ref=src, dst_ref=dst, send_sem=ssem, recv_sem=rsem, device_id=(dp, dq), device_id_type=MESH
            ).start()

        def finish():
            @pl.when(jnp.logical_not(here))
            def _():
                arrived(src, ssem)

        return finish

    tp, hi = q % NP, q // NP
    owner = tp == p

    def level0_q(jb):
        return (jb % 4) * 4 + jb // 4

    @pl.when(owner)
    def _():
        for r in range(8):
            send(lower_hbm.at[r], linv0, l0_s.at[r], l0_r, p, level0_q(2 * r + hi))

    for s in range(2):
        @pl.when(p < 4)
        def _():
            send(rhs_t.at[s], b0, b_s.at[s], b0_r, 2 * z + s, x * 4 + p)

        @pl.when(p >= 4)
        def _():
            send(rhs_t.at[s], bx.at[hi], b_s.at[s], bx_r, p, 2 * tp + s)

    def spread_rhs(finish):
        for at, count, dst, sem in ((4, 2, b1, 0), (5, 2, b1, 0), (6, 4, b2, 1), (7, 4, b3, 2)):
            @pl.when(p == at)
            def _():
                for slot in range(2):
                    r = 2 * at + slot - (8, 12, 14)[sem]
                    rows = H // count
                    for c in range(count):
                        for h in range(2):
                            src = bx.at[slot, pl.ds(h * H + c * rows, rows)]
                            d = 2 * r + c if count == 2 else 2 * c + r
                            ssem = bl_s.at[(slot * count + c) * 2 + h]
                            if finish:
                                @pl.when(p != d)
                                def _():
                                    arrived(src, ssem)
                            else:
                                send(src, dst.at[h], ssem, bl_r.at[sem], d, q)

    def mask_group(g):
        r0, r1, c0, c1 = GROUPS[g]
        loads[g].wait()

        def row(i, carry):
            for j in range(c0, c1):
                keep = jnp.where(pattern[i, j] > 0, 1.0, 0.0).astype(F32)
                m = jnp.full((S, S), keep, F32).astype(BF)
                fm[pl.ds(pl.multiple_of(i * S, S), S), j * S:(j + 1) * S] = raw[i, j] * m
            return carry

        lax.fori_loop(r0, r1, row, 0)

    done = []

    W = 4 * S
    y = p // 2

    def slabs(t, row, col, dst):
        mine = pl.ds(pl.multiple_of(p * W, W), W)

        def push(core, sem, dp, a0, a1):
            pltpu.make_async_remote_copy(
                src_ref=fm.at[pl.ds(pl.multiple_of((row + core) * S + a0, H), a1 - a0), col * S:col * S + W],
                dst_ref=dst.at[a0:a1, mine],
                send_sem=up_s.at[t], recv_sem=up_r.at[t, sem], device_id=(dp, q), device_id_type=MESH,
            ).start()

        for first in (True, False):
            for core in (0, 1):
                for sem, step in ((1, 1), (2, 3)):
                    a0 = H * ((sem == 2) == first)
                    push(core, sem if first else 0, (y + step) % 4 * 2 + core, a0, a0 + H)
        push(1 - p % 2, 0, p + 1 - 2 * (p % 2), 0, S)
        own = fm.at[pl.ds(pl.multiple_of((row + p % 2) * S, S), S), col * S:col * S + W]
        pltpu.make_async_copy(own, dst.at[:, mine], up_r.at[t, 0]).start()
        done.append(lambda: arrived(dst.at[:, 0:7 * W], up_s.at[t]))

    def relay(t, dst):
        for step, sem, a0 in ((1, 1, 0), (3, 2, H)):
            lanes = pl.ds(pl.multiple_of((y + 4 - step) % 4 * 2 * W, 2 * W), 2 * W)
            part = dst.at[a0:a0 + H, lanes]
            arrived(part, up_r.at[t, sem])
            pltpu.make_async_remote_copy(
                src_ref=part, dst_ref=part, send_sem=up_s.at[t], recv_sem=up_r.at[t, 3],
                device_id=((y + step) % 4 * 2 + p % 2, q), device_id_type=MESH,
            ).start()

    def whole(t, dst):
        arrived(dst.at[:, 0:4 * W], up_r.at[t, 0])
        arrived(dst.at[:, 0:2 * W], up_r.at[t, 3])

    mask_group(0)
    slabs(0, 14, 24, up)
    mask_group(1)

    def multicast(h, idx, stage, buf, col, n0, rows, to):
        dst = buf.at[h, pl.ds(n0, rows), pl.ds(pl.multiple_of(col * S, S), S)]
        for dx, dz in STEPS:
            pltpu.make_async_remote_copy(
                src_ref=stage, dst_ref=dst, send_sem=mc_s.at[h, idx], recv_sem=mc_r.at[h, idx],
                device_id=(to, (x + dx) % 4 * 4 + (z + dz) % 4), device_id_type=MESH,
            ).start()
        first = send(stage, dst, mc_s0.at[h, idx], mc_r.at[h, idx], to, q)

        def finish():
            first()
            arrived(fm.at[0:(NQ - 1) * rows, 0:S], mc_s.at[h, idx])

        done.append(finish)

    def to_plane(h, idx, stage, buf):
        col = tp * 4 + 2 * (p % 2) + hi
        dst = buf.at[h, :, pl.ds(pl.multiple_of(col * S, S), S)]
        for dx, dz in STEPS + [(0, 0)]:
            for other in (0, 1):
                if other or dx or dz:
                    pltpu.make_async_remote_copy(
                        src_ref=stage, dst_ref=dst, send_sem=mc_s.at[h, idx], recv_sem=mc_r.at[h, idx],
                        device_id=(p + other * (1 - 2 * (p % 2)), (x + dx) % 4 * 4 + (z + dz) % 4), device_id_type=MESH,
                    ).start()
        pltpu.make_async_copy(stage, dst, mc_r.at[h, idx]).start()
        done.append(lambda: arrived(fm.at[0:31 * 16, 0:S], mc_s.at[h, idx]))

    def exchange(h, idx, ps, rb):
        for k in (4, 5, 3, 2, 6, 7, 1):
            d = (p + k) % NP
            pltpu.make_async_remote_copy(
                src_ref=ps.at[h, d], dst_ref=rb.at[h, k - 1], send_sem=rs_s.at[h, idx], recv_sem=rs_r.at[h, idx],
                device_id=(d, q), device_id_type=MESH,
            ).start()
        done.append(lambda: arrived(rb.at[h], rs_s.at[h, idx]))

    def summed(h, idx, ps, rb):
        arrived(rb.at[h], rs_r.at[h, idx])
        total = ps[h, p].astype(F32)
        for k in range(NP - 1):
            total = total + rb[h, k].astype(F32)
        return total

    def split(h, part, ps, per_row):
        rows = H // per_row
        for d in range(NP):
            r, c = (d // 2, d % 2) if per_row == 2 else (d % 2, d // 2)
            ps[h, d] = part[c * rows:(c + 1) * rows, r * S:(r + 1) * S].astype(BF)

    def cols(ref, h, c0, c1):
        return ref[h, :, c0 * S:c1 * S]

    def blocks(r0, r1, c0, c1):
        return fm[r0 * S:r1 * S, c0 * S:c1 * S]

    def to_output(h, lev, stage, slot_row, n0, rows):
        done.append(send(
            stage, xo.at[q % 2, pl.ds(h * H + n0, rows)], xo_s.at[h, lev], xo_r, slot_row // 2, 8 * (slot_row % 2) + q // 2
        ))

    n1 = pl.multiple_of((p % 2) * 32, 32)
    n2 = pl.multiple_of((p // 2) * 16, 16)

    def chain(h):
        lead = h == 0
        if lead:
            arrived(b0, b0_r)
            arrived(linv0, l0_r)
        y0s[h] = nt(b0[h * H:(h + 1) * H, :], linv0[...]).astype(BF)
        multicast(h, 0, y0s.at[h], yt, z * 4 + x, 0, H, p)
        yield
        if lead:
            @pl.when(p >= 4)
            def _():
                arrived(bx, bx_r)
            spread_rhs(False)
            relay(0, up)
            mask_group(2)
            mask_group(3)
        arrived(yt.at[h, :, 0:16 * S], mc_r.at[h, 0])
        split(h, nt(cols(yt, h, 0, 16), blocks(8, 12, 0, 16)), ps1, 2)
        exchange(h, 0, ps1, rb1)
        yield
        @pl.when(owner)
        def _():
            for d in range(NP):
                col = 2 * level0_row(d) + hi
                send(yt.at[h, :, pl.ds(pl.multiple_of(col * S, S), S)], y0own.at[h], yo_s.at[h, d], yo_r.at[h], d, q)

        accf[h] = nt(cols(yt, h, 0, 16), blocks(12, 16, 0, 16))
        if lead:
            for c in inv_loads:
                c.wait()
            arrived(b1, bl_r.at[0])
        e = (b1[h].astype(F32) - summed(h, 0, ps1, rb1)).astype(BF)
        y1s[h] = nt(e, linv[0]).astype(BF)
        multicast(h, 1, y1s.at[h], yt, 2 * row1 + hi, n1, 32, tp)
        yield
        if lead:
            for g in (4, 5):
                mask_group(g)
        arrived(yt.at[h, :, 16 * S:24 * S], mc_r.at[h, 1])
        split(h, accf[h, :, 0:2 * S] + nt(cols(yt, h, 16, 24), blocks(12, 14, 16, 24)), ps2, 4)
        exchange(h, 1, ps2, rb2)
        split(h, accf[h, :, 2 * S:4 * S] + nt(cols(yt, h, 16, 24), blocks(14, 16, 16, 24)), ps3, 4)
        exchange(h, 2, ps3, rb3)
        yield
        if lead:
            arrived(b2, bl_r.at[1])
        e = (b2[h].astype(F32) - summed(h, 1, ps2, rb2)).astype(BF)
        y2s[h] = nt(e, linv[1]).astype(BF)
        to_plane(h, 2, y2s.at[h], y2p)
        if lead:
            slabs(1, 12, 28, down)
            arrived(b3, bl_r.at[2])
        rest = b3[h].astype(F32) - summed(h, 2, ps3, rb3)
        yield
        if lead:
            relay(1, down)
            whole(0, up)
        arrived(y2p.at[h], mc_r.at[h, 2])
        e = (rest - nt(y2p[h], up[...])).astype(BF)
        y3s[h] = nt(e, linv[2]).astype(BF)
        x3s[h] = nt(y3s[h], uinv[2]).astype(BF)
        to_plane(h, 6, x3s.at[h], x3p)
        yield
        multicast(h, 3, x3s.at[h], xt, 2 * row3 + hi - 16, n2, 16, tp)
        to_output(h, 3, x3s.at[h], row3, n2, 16)
        if lead:
            whole(1, down)
        arrived(x3p.at[h], mc_r.at[h, 6])
        g = (y2s[h].astype(F32) - nt(x3p[h], down[...])).astype(BF)
        x2s[h] = nt(g, uinv[1]).astype(BF)
        multicast(h, 4, x2s.at[h], xt, 2 * row2 + hi - 16, n2, 16, tp)
        to_output(h, 2, x2s.at[h], row2, n2, 16)
        yield
        arrived(xt.at[h, :, 12 * S:16 * S], mc_r.at[h, 3])
        acc1[h] = nt(cols(xt, h, 12, 16), blocks(8, 12, 28, 32))
        acc0[h] = nt(cols(xt, h, 12, 16), blocks(0, 8, 28, 32))
        arrived(xt.at[h, :, 8 * S:12 * S], mc_r.at[h, 4])
        split(h, acc1[h] + nt(cols(xt, h, 8, 12), blocks(8, 12, 24, 28)), psb1, 2)
        exchange(h, 3, psb1, rbb1)
        yield
        acc0[h] += nt(cols(xt, h, 8, 12), blocks(0, 8, 24, 28))
        g = (y1s[h].astype(F32) - summed(h, 3, psb1, rbb1)).astype(BF)
        x1s[h] = nt(g, uinv[0]).astype(BF)
        multicast(h, 5, x1s.at[h], xt, 2 * row1 + hi - 16, n1, 32, tp)
        to_output(h, 1, x1s.at[h], row1, n1, 32)
        yield
        arrived(xt.at[h, :, 0:8 * S], mc_r.at[h, 5])
        part = acc0[h] + nt(cols(xt, h, 0, 8), blocks(0, 8, 16, 24))
        for d in range(NP):
            r = level0_row(d)
            ps0[h, d] = part[:, r * S:(r + 1) * S].astype(BF)
        exchange(h, 4, ps0, rb0)
        yield
        arrived(y0own.at[h], yo_r.at[h])
        g = (y0own[h].astype(F32) - summed(h, 4, ps0, rb0)).astype(BF)
        x0s[h] = nt(g, uinv[3]).astype(BF)
        to_output(h, 0, x0s.at[h], row0, 0, H)
        yield

    chains = [chain(0), chain(1)]
    while chains:
        for c in list(chains):
            try:
                next(c)
            except StopIteration:
                chains.remove(c)

    arrived(xo, xo_r)
    for s in range(2):
        out_ref[s * S:(s + 1) * S, :] = xo[s].astype(F32).T.astype(BF)

    for f in done:
        f()

    @pl.when(owner)
    def _():
        for r in range(8):
            @pl.when(level0_q(2 * r + hi) != q)
            def _():
                arrived(linv0, l0_s.at[r])

        for d in range(NP):
            @pl.when(d != p)
            def _():
                for h in range(2):
                    arrived(y0own.at[h], yo_s.at[h, d])

    for s in range(2):
        @pl.when((p < 4) & jnp.logical_not((2 * z + s == p) & (p == z)))
        def _():
            arrived(b0, b_s.at[s])

        @pl.when((p >= 4) & (2 * tp + s != q))
        def _():
            arrived(b0, b_s.at[s])

    spread_rhs(True)


def on_device(right_sides, factor, pattern, lower_inverse, upper_inverse):
    def vm(*shape, dtype=BF):
        return pltpu.VMEM(shape, dtype)

    dma = pltpu.SemaphoreType.DMA
    hbm = pl.BlockSpec(memory_space=pl.ANY)
    return pl.pallas_call(
        kernel,
        out_shape=jax.ShapeDtypeStruct(right_sides.shape, BF),
        in_specs=[hbm, hbm, pl.BlockSpec(memory_space=pltpu.SMEM), hbm, hbm],
        out_specs=pl.BlockSpec(memory_space=pltpu.VMEM),
        scratch_shapes=[
            vm(16, 32, S, S), vm(16 * S, 32 * S), vm(2, H, 24 * S), vm(2, H, 16 * S),
            vm(2 * S, S), vm(2, S, S),
            vm(S, S), vm(2, S, S), vm(2, 32, S), vm(2, 16, S), vm(2, 16, S),
            vm(S, S), vm(3, S, S), vm(4, S, S),
            vm(2, 8, 32, S), vm(2, 8, 16, S), vm(2, 8, 16, S), vm(2, 8, 32, S), vm(2, 8, H, S),
            vm(2, 7, 32, S), vm(2, 7, 16, S), vm(2, 7, 16, S), vm(2, 7, 32, S), vm(2, 7, H, S),
            vm(S, 32 * S), vm(S, 32 * S), vm(2, 16, 32 * S), vm(2, 16, 32 * S),
            vm(2, H, S), vm(2, 32, S), vm(2, 16, S), vm(2, 16, S),
            vm(2, 16, S), vm(2, 16, S), vm(2, 32, S), vm(2, H, S),
            vm(2, H, S), vm(2, S, S),
            vm(2, H, 4 * S, dtype=F32), vm(2, H, 4 * S, dtype=F32), vm(2, H, 8 * S, dtype=F32),
            dma, dma((6,)), dma((7,)), dma((2,)), dma((2, 4)), dma((2, 5)), dma((2, 5)), dma((2, 7)), dma((2, 7)), dma((2, 7)),
            dma((8,)), dma, dma((2,)), dma, dma, dma((16,)), dma((3,)), dma((2, 8)), dma((2,)), dma((2, 4)), dma,
        ],
        compiler_params=pltpu.CompilerParams(
            collective_id=0, has_side_effects=True, vmem_limit_bytes=60 * 1024 * 1024
        ),
    )(
        right_sides,
        factor.reshape(16, 32, S, S),
        pattern.reshape(16, 32),
        lower_inverse.reshape(16, S, S),
        upper_inverse.reshape(16, S, S),
    )


def solution(mesh):
    return jax.shard_map(
        on_device,
        mesh=mesh,
        in_specs=(
            P(("prow", "pcol"), None),
            P(None, "pcol", None, "prow", None, None),
            P(None, "pcol", None, "prow"),
            P(None, "pcol", None, None),
            P(None, "pcol", None, None),
        ),
        out_specs=P(("prow", "pcol"), None),
        check_vma=False,
    )
```

```python
import jax
import jax.numpy as jnp
from jax import lax
from jax.experimental import pallas as pl
from jax.experimental.pallas import tpu as pltpu
from jax.sharding import PartitionSpec as P

MESH = pl.DeviceIdType.MESH
S = 128
H = 64
BF = jnp.bfloat16
F32 = jnp.float32
NP, NQ = 8, 16

GROUPS = ((14, 16, 24, 28), (8, 16, 0, 16), (12, 16, 16, 24), (12, 14, 28, 32), (8, 12, 24, 32), (0, 8, 16, 32))
STEPS = sorted(
    ((dx, dz) for dx in range(4) for dz in range(4) if dx or dz),
    key=lambda s: -(min(s[0], 4 - s[0]) + min(s[1], 4 - s[1])),
)


def nt(a, b):
    return lax.dot_general(a, b, (((1,), (1,)), ((), ())), preferred_element_type=F32)


def level0_row(p):
    y = p // 2
    return 2 * ((2 * y - y // 2) % 4) + p % 2


def kernel(
    rhs_hbm, factor_hbm, pattern, lower_hbm, upper_hbm, xo,
    raw, fm, yt, xt, rhs_v, rhs_t, b0, bx, b1, b2, b3, linv0, lfirst, linv, uinv,
    ps1, ps2, ps3, psb1, ps0, rb1, rb2, rb3, rbb1, rb0, up, down, y2p, x3p,
    y0s, y1s, y2s, y3s, x3s, x2s, x1s, x0s, y0own, accf, acc1, acc0,
    lsem, fsem, gsem, isem, up_s, up_r, rs_s, rs_r, mc_s, mc_s0, mc_r, l0_s, l0_r, b_s, b0_r, bx_r, bl_s, bl_r, yo_s, yo_r, xo_s, xo_r,
):
    p = lax.axis_index("prow")
    q = lax.axis_index("pcol")
    x, z = q // 4, q % 4
    me = p * NQ + q
    row1, row2, row3, row0 = 8 + p // 2, 12 + p % 2, 14 + p % 2, level0_row(p)

    barrier = pltpu.get_barrier_semaphore()

    def greet(dp, dq):
        pl.semaphore_signal(barrier, 1, device_id=(dp, dq), device_id_type=MESH)

    for dx, dz in STEPS:
        greet(p, (x + dx) % 4 * 4 + (z + dz) % 4)
    for k in range(1, NP):
        greet((p + k) % NP, q)
    corner = (p == 0) & (z == 0)

    @pl.when(jnp.logical_not(corner))
    def _():
        greet(z, x * 4 + p // 2)

    load_rhs = pltpu.make_async_copy(rhs_hbm, rhs_v, lsem)
    load_rhs.start()
    load_first = pltpu.make_async_copy(lower_hbm.at[0:8], lfirst, fsem)
    owner = q % NP == p

    @pl.when(owner)
    def _():
        load_first.start()

    loads = []
    for g, (r0, r1, c0, c1) in enumerate(GROUPS):
        c = pltpu.make_async_copy(factor_hbm.at[r0:r1, c0:c1], raw.at[r0:r1, c0:c1], gsem.at[g])
        c.start()
        loads.append(c)
    inv_loads = []
    for k, r in enumerate((row1, row2, row3)):
        inv_loads.append(pltpu.make_async_copy(lower_hbm.at[r], linv.at[k], isem.at[k]))
    for k, r in enumerate((row1, row2, row3, row0)):
        inv_loads.append(pltpu.make_async_copy(upper_hbm.at[r], uinv.at[k], isem.at[3 + k]))
    for c in inv_loads:
        c.start()

    load_rhs.wait()
    for s in range(2):
        rhs_t[s] = rhs_v[s * S:(s + 1) * S, :].astype(F32).T.astype(BF)

    @pl.when(owner)
    def _():
        load_first.wait()

    pl.semaphore_wait(
        barrier, 22 + jnp.where(p < 4, 2, 0) - jnp.where(corner, 1, 0)
    )

    def arrived(ref, sem):
        pltpu.make_async_copy(ref, ref, sem).wait()

    def send(src, dst, ssem, rsem, dp, dq):
        here = (dp == p) & (dq == q)

        @pl.when(here)
        def _():
            pltpu.make_async_copy(src, dst, rsem).start()

        @pl.when(jnp.logical_not(here))
        def _():
            pltpu.make_async_remote_copy(
                src_ref=src, dst_ref=dst, send_sem=ssem, recv_sem=rsem, device_id=(dp, dq), device_id_type=MESH
            ).start()

        def finish():
            @pl.when(jnp.logical_not(here))
            def _():
                arrived(src, ssem)

        return finish

    tp, hi = q % NP, q // NP

    def level0_q(jb):
        return (jb % 4) * 4 + jb // 4

    @pl.when(owner)
    def _():
        for r in range(8):
            send(lfirst.at[r], linv0, l0_s.at[r], l0_r, p, level0_q(2 * r + hi))

    for s in range(2):
        @pl.when(p < 4)
        def _():
            send(rhs_t.at[s], b0, b_s.at[s], b0_r, 2 * z + s, x * 4 + p)

        @pl.when(p >= 4)
        def _():
            send(rhs_t.at[s], bx.at[hi], b_s.at[s], bx_r, p, 2 * tp + s)

    def spread_rhs(finish):
        for at, count, dst, sem in ((4, 2, b1, 0), (5, 2, b1, 0), (6, 4, b2, 1), (7, 4, b3, 2)):
            @pl.when(p == at)
            def _():
                for slot in range(2):
                    r = 2 * at + slot - (8, 12, 14)[sem]
                    rows = H // count
                    for c in range(count):
                        for h in range(2):
                            src = bx.at[slot, pl.ds(h * H + c * rows, rows)]
                            d = 2 * r + c if count == 2 else 2 * c + r
                            ssem = bl_s.at[(slot * count + c) * 2 + h]
                            if finish:
                                @pl.when(p != d)
                                def _():
                                    arrived(src, ssem)
                            else:
                                send(src, dst.at[h], ssem, bl_r.at[sem], d, q)

    def mask_group(g):
        r0, r1, c0, c1 = GROUPS[g]
        loads[g].wait()

        def row(i, carry):
            for j in range(c0, c1):
                keep = jnp.where(pattern[i, j] > 0, 1.0, 0.0).astype(F32)
                m = jnp.full((S, S), keep, F32).astype(BF)
                fm[pl.ds(pl.multiple_of(i * S, S), S), j * S:(j + 1) * S] = raw[i, j] * m
            return carry

        lax.fori_loop(r0, r1, row, 0)

    done = []

    W = 4 * S
    y = p // 2

    def slabs(t, row, col, dst):
        mine = pl.ds(pl.multiple_of(p * W, W), W)

        def push(core, sem, dp, a0, a1):
            pltpu.make_async_remote_copy(
                src_ref=fm.at[pl.ds(pl.multiple_of((row + core) * S + a0, H), a1 - a0), col * S:col * S + W],
                dst_ref=dst.at[a0:a1, mine],
                send_sem=up_s.at[t], recv_sem=up_r.at[t, sem], device_id=(dp, q), device_id_type=MESH,
            ).start()

        for first in (True, False):
            for core in (0, 1):
                for sem, step in ((1, 1), (2, 3)):
                    a0 = H * ((sem == 2) == first)
                    push(core, sem if first else 0, (y + step) % 4 * 2 + core, a0, a0 + H)
        push(1 - p % 2, 0, p + 1 - 2 * (p % 2), 0, S)
        own = fm.at[pl.ds(pl.multiple_of((row + p % 2) * S, S), S), col * S:col * S + W]
        pltpu.make_async_copy(own, dst.at[:, mine], up_r.at[t, 0]).start()
        done.append(lambda: arrived(dst.at[:, 0:7 * W], up_s.at[t]))

    def relay(t, dst):
        for step, sem, a0 in ((1, 1, 0), (3, 2, H)):
            lanes = pl.ds(pl.multiple_of((y + 4 - step) % 4 * 2 * W, 2 * W), 2 * W)
            part = dst.at[a0:a0 + H, lanes]
            arrived(part, up_r.at[t, sem])
            pltpu.make_async_remote_copy(
                src_ref=part, dst_ref=part, send_sem=up_s.at[t], recv_sem=up_r.at[t, 3],
                device_id=((y + step) % 4 * 2 + p % 2, q), device_id_type=MESH,
            ).start()

    def whole(t, dst):
        arrived(dst.at[:, 0:4 * W], up_r.at[t, 0])
        arrived(dst.at[:, 0:2 * W], up_r.at[t, 3])

    mask_group(0)
    slabs(0, 14, 24, up)
    mask_group(1)

    def multicast(h, idx, stage, buf, col, n0, rows, to):
        dst = buf.at[h, pl.ds(n0, rows), pl.ds(pl.multiple_of(col * S, S), S)]
        for dx, dz in STEPS:
            pltpu.make_async_remote_copy(
                src_ref=stage, dst_ref=dst, send_sem=mc_s.at[h, idx], recv_sem=mc_r.at[h, idx],
                device_id=(to, (x + dx) % 4 * 4 + (z + dz) % 4), device_id_type=MESH,
            ).start()
        first = send(stage, dst, mc_s0.at[h, idx], mc_r.at[h, idx], to, q)

        def finish():
            first()
            arrived(fm.at[0:(NQ - 1) * rows, 0:S], mc_s.at[h, idx])

        done.append(finish)

    def to_plane(h, idx, stage, buf):
        col = tp * 4 + 2 * (p % 2) + hi
        dst = buf.at[h, :, pl.ds(pl.multiple_of(col * S, S), S)]
        for dx, dz in STEPS + [(0, 0)]:
            for other in (0, 1):
                if other or dx or dz:
                    pltpu.make_async_remote_copy(
                        src_ref=stage, dst_ref=dst, send_sem=mc_s.at[h, idx], recv_sem=mc_r.at[h, idx],
                        device_id=(p + other * (1 - 2 * (p % 2)), (x + dx) % 4 * 4 + (z + dz) % 4), device_id_type=MESH,
                    ).start()
        pltpu.make_async_copy(stage, dst, mc_r.at[h, idx]).start()
        done.append(lambda: arrived(fm.at[0:31 * 16, 0:S], mc_s.at[h, idx]))

    def exchange(h, idx, ps, rb):
        for k in (4, 5, 3, 2, 6, 7, 1):
            d = (p + k) % NP
            pltpu.make_async_remote_copy(
                src_ref=ps.at[h, d], dst_ref=rb.at[h, k - 1], send_sem=rs_s.at[h, idx], recv_sem=rs_r.at[h, idx],
                device_id=(d, q), device_id_type=MESH,
            ).start()
        done.append(lambda: arrived(rb.at[h], rs_s.at[h, idx]))

    def summed(h, idx, ps, rb):
        arrived(rb.at[h], rs_r.at[h, idx])
        total = ps[h, p].astype(F32)
        for k in range(NP - 1):
            total = total + rb[h, k].astype(F32)
        return total

    def split(h, part, ps, per_row):
        rows = H // per_row
        for d in range(NP):
            r, c = (d // 2, d % 2) if per_row == 2 else (d % 2, d // 2)
            ps[h, d] = part[c * rows:(c + 1) * rows, r * S:(r + 1) * S].astype(BF)

    def cols(ref, h, c0, c1):
        return ref[h, :, c0 * S:c1 * S]

    def blocks(r0, r1, c0, c1):
        return fm[r0 * S:r1 * S, c0 * S:c1 * S]

    def to_output(h, lev, stage, slot_row, n0, rows):
        done.append(send(
            stage, xo.at[q % 2, pl.ds(h * H + n0, rows)], xo_s.at[h, lev], xo_r, slot_row // 2, 8 * (slot_row % 2) + q // 2
        ))

    n1 = pl.multiple_of((p % 2) * 32, 32)
    n2 = pl.multiple_of((p // 2) * 16, 16)

    def chain(h):
        lead = h == 0
        if lead:
            arrived(b0, b0_r)
            arrived(linv0, l0_r)
        y0s[h] = nt(b0[h * H:(h + 1) * H, :], linv0[...]).astype(BF)
        multicast(h, 0, y0s.at[h], yt, z * 4 + x, 0, H, p)
        yield
        if lead:
            @pl.when(p >= 4)
            def _():
                arrived(bx, bx_r)
            spread_rhs(False)
            relay(0, up)
            mask_group(2)
            mask_group(3)
        arrived(yt.at[h, :, 0:16 * S], mc_r.at[h, 0])
        split(h, nt(cols(yt, h, 0, 16), blocks(8, 12, 0, 16)), ps1, 2)
        exchange(h, 0, ps1, rb1)
        yield
        @pl.when(owner)
        def _():
            for d in range(NP):
                col = 2 * level0_row(d) + hi
                send(yt.at[h, :, pl.ds(pl.multiple_of(col * S, S), S)], y0own.at[h], yo_s.at[h, d], yo_r.at[h], d, q)

        accf[h] = nt(cols(yt, h, 0, 16), blocks(12, 16, 0, 16))
        if lead:
            for c in inv_loads:
                c.wait()
            arrived(b1, bl_r.at[0])
        e = (b1[h].astype(F32) - summed(h, 0, ps1, rb1)).astype(BF)
        y1s[h] = nt(e, linv[0]).astype(BF)
        multicast(h, 1, y1s.at[h], yt, 2 * row1 + hi, n1, 32, tp)
        yield
        if lead:
            for g in (4, 5):
                mask_group(g)
        arrived(yt.at[h, :, 16 * S:24 * S], mc_r.at[h, 1])
        split(h, accf[h, :, 0:2 * S] + nt(cols(yt, h, 16, 24), blocks(12, 14, 16, 24)), ps2, 4)
        exchange(h, 1, ps2, rb2)
        split(h, accf[h, :, 2 * S:4 * S] + nt(cols(yt, h, 16, 24), blocks(14, 16, 16, 24)), ps3, 4)
        exchange(h, 2, ps3, rb3)
        yield
        if lead:
            arrived(b2, bl_r.at[1])
        e = (b2[h].astype(F32) - summed(h, 1, ps2, rb2)).astype(BF)
        y2s[h] = nt(e, linv[1]).astype(BF)
        to_plane(h, 2, y2s.at[h], y2p)
        if lead:
            slabs(1, 12, 28, down)
            arrived(b3, bl_r.at[2])
        rest = b3[h].astype(F32) - summed(h, 2, ps3, rb3)
        yield
        if lead:
            relay(1, down)
            whole(0, up)
        arrived(y2p.at[h], mc_r.at[h, 2])
        e = (rest - nt(y2p[h], up[...])).astype(BF)
        y3s[h] = nt(e, linv[2]).astype(BF)
        x3s[h] = nt(y3s[h], uinv[2]).astype(BF)
        to_plane(h, 6, x3s.at[h], x3p)
        yield
        multicast(h, 3, x3s.at[h], xt, 2 * row3 + hi - 16, n2, 16, tp)
        to_output(h, 3, x3s.at[h], row3, n2, 16)
        if lead:
            whole(1, down)
        arrived(x3p.at[h], mc_r.at[h, 6])
        g = (y2s[h].astype(F32) - nt(x3p[h], down[...])).astype(BF)
        x2s[h] = nt(g, uinv[1]).astype(BF)
        multicast(h, 4, x2s.at[h], xt, 2 * row2 + hi - 16, n2, 16, tp)
        to_output(h, 2, x2s.at[h], row2, n2, 16)
        yield
        arrived(xt.at[h, :, 12 * S:16 * S], mc_r.at[h, 3])
        acc1[h] = nt(cols(xt, h, 12, 16), blocks(8, 12, 28, 32))
        acc0[h] = nt(cols(xt, h, 12, 16), blocks(0, 8, 28, 32))
        arrived(xt.at[h, :, 8 * S:12 * S], mc_r.at[h, 4])
        split(h, acc1[h] + nt(cols(xt, h, 8, 12), blocks(8, 12, 24, 28)), psb1, 2)
        exchange(h, 3, psb1, rbb1)
        yield
        acc0[h] += nt(cols(xt, h, 8, 12), blocks(0, 8, 24, 28))
        g = (y1s[h].astype(F32) - summed(h, 3, psb1, rbb1)).astype(BF)
        x1s[h] = nt(g, uinv[0]).astype(BF)
        multicast(h, 5, x1s.at[h], xt, 2 * row1 + hi - 16, n1, 32, tp)
        to_output(h, 1, x1s.at[h], row1, n1, 32)
        yield
        arrived(xt.at[h, :, 0:8 * S], mc_r.at[h, 5])
        part = acc0[h] + nt(cols(xt, h, 0, 8), blocks(0, 8, 16, 24))
        for d in range(NP):
            r = level0_row(d)
            ps0[h, d] = part[:, r * S:(r + 1) * S].astype(BF)
        exchange(h, 4, ps0, rb0)
        yield
        arrived(y0own.at[h], yo_r.at[h])
        g = (y0own[h].astype(F32) - summed(h, 4, ps0, rb0)).astype(BF)
        x0s[h] = nt(g, uinv[3]).astype(BF)
        to_output(h, 0, x0s.at[h], row0, 0, H)
        yield

    chains = [chain(0), chain(1)]
    while chains:
        for c in list(chains):
            try:
                next(c)
            except StopIteration:
                chains.remove(c)

    for f in done:
        f()

    @pl.when(owner)
    def _():
        for r in range(8):
            @pl.when(level0_q(2 * r + hi) != q)
            def _():
                arrived(linv0, l0_s.at[r])

        for d in range(NP):
            @pl.when(d != p)
            def _():
                for h in range(2):
                    arrived(y0own.at[h], yo_s.at[h, d])

    for s in range(2):
        @pl.when((p < 4) & jnp.logical_not((2 * z + s == p) & (p == z)))
        def _():
            arrived(b0, b_s.at[s])

        @pl.when((p >= 4) & (2 * tp + s != q))
        def _():
            arrived(b0, b_s.at[s])

    spread_rhs(True)

    arrived(xo, xo_r)


def on_device(right_sides, factor, pattern, lower_inverse, upper_inverse):
    def vm(*shape, dtype=BF):
        return pltpu.VMEM(shape, dtype)

    dma = pltpu.SemaphoreType.DMA
    hbm = pl.BlockSpec(memory_space=pl.ANY)
    solved = pl.pallas_call(
        kernel,
        out_shape=jax.ShapeDtypeStruct((2, S, S), BF),
        in_specs=[hbm, hbm, pl.BlockSpec(memory_space=pltpu.SMEM), hbm, hbm],
        out_specs=hbm,
        scratch_shapes=[
            vm(16, 32, S, S), vm(16 * S, 32 * S), vm(2, H, 24 * S), vm(2, H, 16 * S),
            vm(2 * S, S), vm(2, S, S),
            vm(S, S), vm(2, S, S), vm(2, 32, S), vm(2, 16, S), vm(2, 16, S),
            vm(S, S), vm(8, S, S), vm(3, S, S), vm(4, S, S),
            vm(2, 8, 32, S), vm(2, 8, 16, S), vm(2, 8, 16, S), vm(2, 8, 32, S), vm(2, 8, H, S),
            vm(2, 7, 32, S), vm(2, 7, 16, S), vm(2, 7, 16, S), vm(2, 7, 32, S), vm(2, 7, H, S),
            vm(S, 32 * S), vm(S, 32 * S), vm(2, 16, 32 * S), vm(2, 16, 32 * S),
            vm(2, H, S), vm(2, 32, S), vm(2, 16, S), vm(2, 16, S),
            vm(2, 16, S), vm(2, 16, S), vm(2, 32, S), vm(2, H, S),
            vm(2, H, S),
            vm(2, H, 4 * S, dtype=F32), vm(2, H, 4 * S, dtype=F32), vm(2, H, 8 * S, dtype=F32),
            dma, dma, dma((6,)), dma((7,)), dma((2,)), dma((2, 4)), dma((2, 5)), dma((2, 5)), dma((2, 7)), dma((2, 7)), dma((2, 7)),
            dma((8,)), dma, dma((2,)), dma, dma, dma((16,)), dma((3,)), dma((2, 8)), dma((2,)), dma((2, 4)), dma,
        ],
        compiler_params=pltpu.CompilerParams(
            collective_id=0, has_side_effects=True, vmem_limit_bytes=60 * 1024 * 1024
        ),
    )(
        right_sides,
        factor.reshape(16, 32, S, S),
        pattern.reshape(16, 32),
        lower_inverse.reshape(16, S, S),
        upper_inverse.reshape(16, S, S),
    )
    return solved.transpose(0, 2, 1).reshape(right_sides.shape)


def solution(mesh):
    return jax.shard_map(
        on_device,
        mesh=mesh,
        in_specs=(
            P(("prow", "pcol"), None),
            P(None, "pcol", None, "prow", None, None),
            P(None, "pcol", None, "prow"),
            P(None, "pcol", None, None),
            P(None, "pcol", None, None),
        ),
        out_specs=P(("prow", "pcol"), None),
        check_vma=False,
    )
```

```python
import jax
import jax.numpy as jnp
from jax import lax
from jax.experimental import pallas as pl
from jax.experimental.pallas import tpu as pltpu
from jax.sharding import PartitionSpec as P

MESH = pl.DeviceIdType.MESH
S = 128
H = 64
BF = jnp.bfloat16
F32 = jnp.float32
NP, NQ = 8, 16

GROUPS = ((14, 16, 24, 28), (8, 16, 0, 16), (12, 16, 16, 24), (12, 14, 28, 32), (8, 12, 24, 32), (0, 8, 16, 32))
STEPS = sorted(
    ((dx, dz) for dx in range(4) for dz in range(4) if dx or dz),
    key=lambda s: -(min(s[0], 4 - s[0]) + min(s[1], 4 - s[1])),
)


def nt(a, b):
    return lax.dot_general(a, b, (((1,), (1,)), ((), ())), preferred_element_type=F32)


def level0_row(p):
    y = p // 2
    return 2 * ((2 * y - y // 2) % 4) + p % 2


def kernel(
    rhs_hbm, factor_hbm, pattern, lower_hbm, upper_hbm, xo,
    raw, fm, yt, xt, rhs_v, rhs_t, b0, bx, b1, b2, b3, linv0, lfirst, linv, uinv,
    ps1, ps2, ps3, psb1, ps0, rb1, rb2, rb3, rbb1, rb0, up, down, y2p, x3p,
    y0s, y1s, y2s, y3s, x3s, x2s, x1s, x0s, y0own, accf, acc1, acc0,
    lsem, fsem, gsem, isem, up_s, up_r, rs_s, rs_r, mc_s, mc_s0, mc_r, l0_s, l0_r, b_s, b0_r, bx_r, bl_s, bl_r, yo_s, yo_r, xo_s, xo_r,
):
    p = lax.axis_index("prow")
    q = lax.axis_index("pcol")
    x, z = q // 4, q % 4
    me = p * NQ + q
    row1, row2, row3, row0 = 8 + p // 2, 12 + p % 2, 14 + p % 2, level0_row(p)

    barrier = pltpu.get_barrier_semaphore()

    def greet(dp, dq):
        pl.semaphore_signal(barrier, 1, device_id=(dp, dq), device_id_type=MESH)

    for dx, dz in STEPS:
        greet(p, (x + dx) % 4 * 4 + (z + dz) % 4)
    for k in range(1, NP):
        greet((p + k) % NP, q)
    corner = (p == 0) & (z == 0)

    @pl.when(jnp.logical_not(corner))
    def _():
        greet(z, x * 4 + p // 2)

    load_rhs = pltpu.make_async_copy(rhs_hbm, rhs_v, lsem)
    load_rhs.start()
    load_first = pltpu.make_async_copy(lower_hbm.at[0:8], lfirst, fsem)
    owner = q % NP == p

    @pl.when(owner)
    def _():
        load_first.start()

    loads = []
    for g, (r0, r1, c0, c1) in enumerate(GROUPS):
        c = pltpu.make_async_copy(factor_hbm.at[r0:r1, c0:c1], raw.at[r0:r1, c0:c1], gsem.at[g])
        c.start()
        loads.append(c)
    inv_loads = []
    for k, r in enumerate((row1, row2, row3)):
        inv_loads.append(pltpu.make_async_copy(lower_hbm.at[r], linv.at[k], isem.at[k]))
    for k, r in enumerate((row1, row2, row3, row0)):
        inv_loads.append(pltpu.make_async_copy(upper_hbm.at[r], uinv.at[k], isem.at[3 + k]))
    for c in inv_loads:
        c.start()

    load_rhs.wait()
    for s in range(2):
        rhs_t[s] = rhs_v[s * S:(s + 1) * S, :].astype(F32).T.astype(BF)

    @pl.when(owner)
    def _():
        load_first.wait()

    pl.semaphore_wait(
        barrier, 22 + jnp.where(p < 4, 2, 0) - jnp.where(corner, 1, 0)
    )

    def arrived(ref, sem):
        pltpu.make_async_copy(ref, ref, sem).wait()

    def send(src, dst, ssem, rsem, dp, dq):
        here = (dp == p) & (dq == q)

        @pl.when(here)
        def _():
            pltpu.make_async_copy(src, dst, rsem).start()

        @pl.when(jnp.logical_not(here))
        def _():
            pltpu.make_async_remote_copy(
                src_ref=src, dst_ref=dst, send_sem=ssem, recv_sem=rsem, device_id=(dp, dq), device_id_type=MESH
            ).start()

        def finish():
            @pl.when(jnp.logical_not(here))
            def _():
                arrived(src, ssem)

        return finish

    tp, hi = q % NP, q // NP

    def level0_q(jb):
        return (jb % 4) * 4 + jb // 4

    @pl.when(owner)
    def _():
        for r in range(8):
            send(lfirst.at[r], linv0, l0_s.at[r], l0_r, p, level0_q(2 * r + hi))

    for s in range(2):
        @pl.when(p < 4)
        def _():
            send(rhs_t.at[s], b0, b_s.at[s], b0_r, 2 * z + s, x * 4 + p)

        @pl.when(p >= 4)
        def _():
            send(rhs_t.at[s], bx.at[hi], b_s.at[s], bx_r, p, 2 * tp + s)

    def spread_rhs(finish):
        for at, count, dst, sem in ((4, 2, b1, 0), (5, 2, b1, 0), (6, 4, b2, 1), (7, 4, b3, 2)):
            @pl.when(p == at)
            def _():
                for slot in range(2):
                    r = 2 * at + slot - (8, 12, 14)[sem]
                    rows = H // count
                    for c in range(count):
                        for h in range(2):
                            src = bx.at[slot, pl.ds(h * H + c * rows, rows)]
                            d = 2 * r + c if count == 2 else 2 * c + r
                            ssem = bl_s.at[(slot * count + c) * 2 + h]
                            if finish:
                                @pl.when(p != d)
                                def _():
                                    arrived(src, ssem)
                            else:
                                send(src, dst.at[h], ssem, bl_r.at[sem], d, q)

    def mask_group(g):
        r0, r1, c0, c1 = GROUPS[g]
        loads[g].wait()

        def row(i, carry):
            for j in range(c0, c1):
                keep = jnp.where(pattern[i, j] > 0, 1.0, 0.0).astype(F32)
                m = jnp.full((S, S), keep, F32).astype(BF)
                fm[pl.ds(pl.multiple_of(i * S, S), S), j * S:(j + 1) * S] = raw[i, j] * m
            return carry

        lax.fori_loop(r0, r1, row, 0)

    done = []

    W = 4 * S
    y = p // 2

    def slabs(t, row, col, dst):
        mine = pl.ds(pl.multiple_of(p * W, W), W)

        def push(core, sem, dp, a0, a1):
            pltpu.make_async_remote_copy(
                src_ref=fm.at[pl.ds(pl.multiple_of((row + core) * S + a0, H), a1 - a0), col * S:col * S + W],
                dst_ref=dst.at[a0:a1, mine],
                send_sem=up_s.at[t], recv_sem=up_r.at[t, sem], device_id=(dp, q), device_id_type=MESH,
            ).start()

        for first in (True, False):
            for core in (0, 1):
                for sem, step in ((1, 1), (2, 3)):
                    a0 = H * ((sem == 2) == first)
                    push(core, sem if first else 0, (y + step) % 4 * 2 + core, a0, a0 + H)
        push(1 - p % 2, 0, p + 1 - 2 * (p % 2), 0, S)
        own = fm.at[pl.ds(pl.multiple_of((row + p % 2) * S, S), S), col * S:col * S + W]
        pltpu.make_async_copy(own, dst.at[:, mine], up_r.at[t, 0]).start()
        done.append(lambda: arrived(dst.at[:, 0:7 * W], up_s.at[t]))

    def relay(t, dst):
        for step, sem, a0 in ((1, 1, 0), (3, 2, H)):
            lanes = pl.ds(pl.multiple_of((y + 4 - step) % 4 * 2 * W, 2 * W), 2 * W)
            part = dst.at[a0:a0 + H, lanes]
            arrived(part, up_r.at[t, sem])
            pltpu.make_async_remote_copy(
                src_ref=part, dst_ref=part, send_sem=up_s.at[t], recv_sem=up_r.at[t, 3],
                device_id=((y + step) % 4 * 2 + p % 2, q), device_id_type=MESH,
            ).start()

    def whole(t, dst):
        arrived(dst.at[:, 0:4 * W], up_r.at[t, 0])
        arrived(dst.at[:, 0:2 * W], up_r.at[t, 3])

    mask_group(0)
    slabs(0, 14, 24, up)
    mask_group(1)

    def multicast(h, idx, stage, buf, col, n0, rows, to):
        dst = buf.at[h, pl.ds(n0, rows), pl.ds(pl.multiple_of(col * S, S), S)]
        for dx, dz in STEPS:
            pltpu.make_async_remote_copy(
                src_ref=stage, dst_ref=dst, send_sem=mc_s.at[h, idx], recv_sem=mc_r.at[h, idx],
                device_id=(to, (x + dx) % 4 * 4 + (z + dz) % 4), device_id_type=MESH,
            ).start()
        first = send(stage, dst, mc_s0.at[h, idx], mc_r.at[h, idx], to, q)

        def finish():
            first()
            arrived(fm.at[0:(NQ - 1) * rows, 0:S], mc_s.at[h, idx])

        done.append(finish)

    def to_plane(h, idx, stage, buf):
        col = tp * 4 + 2 * (p % 2) + hi
        dst = buf.at[h, :, pl.ds(pl.multiple_of(col * S, S), S)]
        for dx, dz in STEPS + [(0, 0)]:
            for other in (0, 1):
                if other or dx or dz:
                    pltpu.make_async_remote_copy(
                        src_ref=stage, dst_ref=dst, send_sem=mc_s.at[h, idx], recv_sem=mc_r.at[h, idx],
                        device_id=(p + other * (1 - 2 * (p % 2)), (x + dx) % 4 * 4 + (z + dz) % 4), device_id_type=MESH,
                    ).start()
        pltpu.make_async_copy(stage, dst, mc_r.at[h, idx]).start()
        done.append(lambda: arrived(fm.at[0:31 * 16, 0:S], mc_s.at[h, idx]))

    def exchange(h, idx, ps, rb):
        for k in (4, 5, 3, 2, 6, 7, 1):
            d = (p + k) % NP
            pltpu.make_async_remote_copy(
                src_ref=ps.at[h, d], dst_ref=rb.at[h, k - 1], send_sem=rs_s.at[h, idx], recv_sem=rs_r.at[h, idx],
                device_id=(d, q), device_id_type=MESH,
            ).start()
        done.append(lambda: arrived(rb.at[h], rs_s.at[h, idx]))

    def summed(h, idx, ps, rb):
        arrived(rb.at[h], rs_r.at[h, idx])
        parts = [ps[h, p].astype(F32)] + [rb[h, k].astype(F32) for k in range(NP - 1)]
        while len(parts) > 1:
            parts = [u + v for u, v in zip(parts[::2], parts[1::2])]
        return parts[0]

    def split(h, part, ps, per_row):
        rows = H // per_row
        for d in range(NP):
            r, c = (d // 2, d % 2) if per_row == 2 else (d % 2, d // 2)
            ps[h, d] = part[c * rows:(c + 1) * rows, r * S:(r + 1) * S].astype(BF)

    def cols(ref, h, c0, c1):
        return ref[h, :, c0 * S:c1 * S]

    def blocks(r0, r1, c0, c1):
        return fm[r0 * S:r1 * S, c0 * S:c1 * S]

    def to_output(h, lev, stage, slot_row, n0, rows):
        done.append(send(
            stage, xo.at[q % 2, pl.ds(h * H + n0, rows)], xo_s.at[h, lev], xo_r, slot_row // 2, 8 * (slot_row % 2) + q // 2
        ))

    n1 = pl.multiple_of((p % 2) * 32, 32)
    n2 = pl.multiple_of((p // 2) * 16, 16)

    def chain(h):
        lead = h == 0
        if lead:
            arrived(b0, b0_r)
            arrived(linv0, l0_r)
        y0s[h] = nt(b0[h * H:(h + 1) * H, :], linv0[...]).astype(BF)
        multicast(h, 0, y0s.at[h], yt, z * 4 + x, 0, H, p)
        yield
        if lead:
            @pl.when(p >= 4)
            def _():
                arrived(bx, bx_r)
            spread_rhs(False)
            relay(0, up)
            mask_group(2)
            mask_group(3)
        arrived(yt.at[h, :, 0:16 * S], mc_r.at[h, 0])
        split(h, nt(cols(yt, h, 0, 16), blocks(8, 12, 0, 16)), ps1, 2)
        exchange(h, 0, ps1, rb1)
        yield
        accf[h] = nt(cols(yt, h, 0, 16), blocks(12, 16, 0, 16))
        if lead:
            for c in inv_loads:
                c.wait()
            arrived(b1, bl_r.at[0])
        e = (b1[h].astype(F32) - summed(h, 0, ps1, rb1)).astype(BF)
        y1s[h] = nt(e, linv[0]).astype(BF)
        multicast(h, 1, y1s.at[h], yt, 2 * row1 + hi, n1, 32, tp)
        @pl.when(owner)
        def _():
            for d in range(NP):
                col = 2 * level0_row(d) + hi
                send(yt.at[h, :, pl.ds(pl.multiple_of(col * S, S), S)], y0own.at[h], yo_s.at[h, d], yo_r.at[h], d, q)

        yield
        if lead:
            for g in (4, 5):
                mask_group(g)
        arrived(yt.at[h, :, 16 * S:24 * S], mc_r.at[h, 1])
        split(h, accf[h, :, 0:2 * S] + nt(cols(yt, h, 16, 24), blocks(12, 14, 16, 24)), ps2, 4)
        exchange(h, 1, ps2, rb2)
        split(h, accf[h, :, 2 * S:4 * S] + nt(cols(yt, h, 16, 24), blocks(14, 16, 16, 24)), ps3, 4)
        exchange(h, 2, ps3, rb3)
        yield
        if lead:
            arrived(b2, bl_r.at[1])
        e = (b2[h].astype(F32) - summed(h, 1, ps2, rb2)).astype(BF)
        y2s[h] = nt(e, linv[1]).astype(BF)
        to_plane(h, 2, y2s.at[h], y2p)
        if lead:
            slabs(1, 12, 28, down)
            arrived(b3, bl_r.at[2])
        rest = b3[h].astype(F32) - summed(h, 2, ps3, rb3)
        yield
        if lead:
            relay(1, down)
            whole(0, up)
        arrived(y2p.at[h], mc_r.at[h, 2])
        e = (rest - nt(y2p[h], up[...])).astype(BF)
        y3s[h] = nt(e, linv[2]).astype(BF)
        x3s[h] = nt(y3s[h], uinv[2]).astype(BF)
        to_plane(h, 6, x3s.at[h], x3p)
        yield
        multicast(h, 3, x3s.at[h], xt, 2 * row3 + hi - 16, n2, 16, tp)
        to_output(h, 3, x3s.at[h], row3, n2, 16)
        if lead:
            whole(1, down)
        arrived(x3p.at[h], mc_r.at[h, 6])
        g = (y2s[h].astype(F32) - nt(x3p[h], down[...])).astype(BF)
        x2s[h] = nt(g, uinv[1]).astype(BF)
        multicast(h, 4, x2s.at[h], xt, 2 * row2 + hi - 16, n2, 16, tp)
        to_output(h, 2, x2s.at[h], row2, n2, 16)
        yield
        arrived(xt.at[h, :, 12 * S:16 * S], mc_r.at[h, 3])
        acc1[h] = nt(cols(xt, h, 12, 16), blocks(8, 12, 28, 32))
        acc0[h] = nt(cols(xt, h, 12, 16), blocks(0, 8, 28, 32))
        arrived(xt.at[h, :, 8 * S:12 * S], mc_r.at[h, 4])
        split(h, acc1[h] + nt(cols(xt, h, 8, 12), blocks(8, 12, 24, 28)), psb1, 2)
        exchange(h, 3, psb1, rbb1)
        yield
        acc0[h] += nt(cols(xt, h, 8, 12), blocks(0, 8, 24, 28))
        g = (y1s[h].astype(F32) - summed(h, 3, psb1, rbb1)).astype(BF)
        x1s[h] = nt(g, uinv[0]).astype(BF)
        multicast(h, 5, x1s.at[h], xt, 2 * row1 + hi - 16, n1, 32, tp)
        to_output(h, 1, x1s.at[h], row1, n1, 32)
        yield
        arrived(xt.at[h, :, 0:8 * S], mc_r.at[h, 5])
        for r0 in (0, 4):
            part = acc0[h, :, r0 * S:(r0 + 4) * S] + nt(cols(xt, h, 0, 8), blocks(r0, r0 + 4, 16, 24))
            for d in range(NP):
                r = level0_row(d) - r0
                if 0 <= r < 4:
                    ps0[h, d] = part[:, r * S:(r + 1) * S].astype(BF)
                    k = (d - p + NP) % NP

                    @pl.when(k > 0)
                    def _():
                        pltpu.make_async_remote_copy(
                            src_ref=ps0.at[h, d], dst_ref=rb0.at[h, k - 1], send_sem=rs_s.at[h, 4], recv_sem=rs_r.at[h, 4],
                            device_id=(d, q), device_id_type=MESH,
                        ).start()
        done.append(lambda: arrived(rb0.at[h], rs_s.at[h, 4]))
        yield
        arrived(y0own.at[h], yo_r.at[h])
        g = (y0own[h].astype(F32) - summed(h, 4, ps0, rb0)).astype(BF)
        x0s[h] = nt(g, uinv[3]).astype(BF)
        to_output(h, 0, x0s.at[h], row0, 0, H)
        yield

    chains = [chain(0), chain(1)]
    while chains:
        for c in list(chains):
            try:
                next(c)
            except StopIteration:
                chains.remove(c)

    for f in done:
        f()

    @pl.when(owner)
    def _():
        for r in range(8):
            @pl.when(level0_q(2 * r + hi) != q)
            def _():
                arrived(linv0, l0_s.at[r])

        for d in range(NP):
            @pl.when(d != p)
            def _():
                for h in range(2):
                    arrived(y0own.at[h], yo_s.at[h, d])

    for s in range(2):
        @pl.when((p < 4) & jnp.logical_not((2 * z + s == p) & (p == z)))
        def _():
            arrived(b0, b_s.at[s])

        @pl.when((p >= 4) & (2 * tp + s != q))
        def _():
            arrived(b0, b_s.at[s])

    spread_rhs(True)

    arrived(xo, xo_r)


def on_device(right_sides, factor, pattern, lower_inverse, upper_inverse):
    def vm(*shape, dtype=BF):
        return pltpu.VMEM(shape, dtype)

    dma = pltpu.SemaphoreType.DMA
    hbm = pl.BlockSpec(memory_space=pl.ANY)
    solved = pl.pallas_call(
        kernel,
        out_shape=jax.ShapeDtypeStruct((2, S, S), BF),
        in_specs=[hbm, hbm, pl.BlockSpec(memory_space=pltpu.SMEM), hbm, hbm],
        out_specs=hbm,
        scratch_shapes=[
            vm(16, 32, S, S), vm(16 * S, 32 * S), vm(2, H, 24 * S), vm(2, H, 16 * S),
            vm(2 * S, S), vm(2, S, S),
            vm(S, S), vm(2, S, S), vm(2, 32, S), vm(2, 16, S), vm(2, 16, S),
            vm(S, S), vm(8, S, S), vm(3, S, S), vm(4, S, S),
            vm(2, 8, 32, S), vm(2, 8, 16, S), vm(2, 8, 16, S), vm(2, 8, 32, S), vm(2, 8, H, S),
            vm(2, 7, 32, S), vm(2, 7, 16, S), vm(2, 7, 16, S), vm(2, 7, 32, S), vm(2, 7, H, S),
            vm(S, 32 * S), vm(S, 32 * S), vm(2, 16, 32 * S), vm(2, 16, 32 * S),
            vm(2, H, S), vm(2, 32, S), vm(2, 16, S), vm(2, 16, S),
            vm(2, 16, S), vm(2, 16, S), vm(2, 32, S), vm(2, H, S),
            vm(2, H, S),
            vm(2, H, 4 * S, dtype=F32), vm(2, H, 4 * S, dtype=F32), vm(2, H, 8 * S, dtype=F32),
            dma, dma, dma((6,)), dma((7,)), dma((2,)), dma((2, 4)), dma((2, 5)), dma((2, 5)), dma((2, 7)), dma((2, 7)), dma((2, 7)),
            dma((8,)), dma, dma((2,)), dma, dma, dma((16,)), dma((3,)), dma((2, 8)), dma((2,)), dma((2, 4)), dma,
        ],
        compiler_params=pltpu.CompilerParams(
            collective_id=0, has_side_effects=True, vmem_limit_bytes=60 * 1024 * 1024
        ),
    )(
        right_sides,
        factor.reshape(16, 32, S, S),
        pattern.reshape(16, 32),
        lower_inverse.reshape(16, S, S),
        upper_inverse.reshape(16, S, S),
    )
    return solved.transpose(0, 2, 1).reshape(right_sides.shape)


def solution(mesh):
    return jax.shard_map(
        on_device,
        mesh=mesh,
        in_specs=(
            P(("prow", "pcol"), None),
            P(None, "pcol", None, "prow", None, None),
            P(None, "pcol", None, "prow"),
            P(None, "pcol", None, None),
            P(None, "pcol", None, None),
        ),
        out_specs=P(("prow", "pcol"), None),
        check_vma=False,
    )
```
